32 devices in a mesh: seq: 4 (over z_hi, core), expert: 4 (over y, x), tensor: 2 (over z_lo).
Axes of the slice: x: 2, y: 2, z: 4 (z_hi: 2, z_lo: 2; z = z_hi * 2 + z_lo), core: 2. Of those that a mesh axis runs over, the one named last changes fastest.
Arguments:
- q_rows: bfloat16 [4, 512, 4096], P('expert', 'seq', 'tensor'), may hold values from -6 to 6
- k_rows: bfloat16 [4, 512, 512], P('expert', 'seq', 'tensor'), may hold values from -6 to 6
- value_rows: bfloat16 [4, 512, 512], P('expert', 'seq', 'tensor'), may hold values from -6 to 6
- x_rows: bfloat16 [4, 512, 2048], P('expert', 'seq'), may hold values from -40 to 40
- out_weight: bfloat16 [4096, 2048], P('tensor', 'expert'), may hold values from -0.09375 to 0.09375
- norm_gain: float32 [2048], P('tensor'), may hold values from 0.1 to 1.9
- w_gate: bfloat16 [16, 2048, 768], P(('seq', 'expert'), None, 'tensor'), may hold values from -0.125 to 0.125
- w_up: bfloat16 [16, 2048, 768], P(('seq', 'expert'), None, 'tensor'), may hold values from -0.125 to 0.125
- w_down: bfloat16 [16, 768, 2048], P(('seq', 'expert'), 'tensor'), may hold values from -0.21875 to 0.21875
- expert_ids: int32 [4, 512, 8], P('expert', 'seq'), may hold values from 0 to 15, all different within a row; in each aligned block of 128 rows (0 to 127, 128 to 255, ..., all dimensions but the last counted through in order) at most 96 rows name the same one
- gate_weights: float32 [4, 512, 8], P('expert', 'seq'), may hold values from 0.02 to 0.4
Outputs:
- layer_out: bfloat16 [4, 512, 2048], P('expert', 'seq', 'tensor')
The draws below stay inside these ranges and needn't reach their ends.
Inputs may be any that keep to these rules, and one draw needn't show every extreme that they name: `expert_ids`: in each token's row the 8 ids differ. Among the 128 tokens of one block of positions (the blocks laid session after session) no expert is named more than 96 times, a bound that some block reaches; every expert is named somewhere.
All inputs are finite; a program needn't handle non-finite values.
Results may differ from the reference program's by a relative error of at most 0.007.
Values may be sent and summed in bfloat16 or wider, within the bound.
No kernel may reach another device: no remote copies, remote signals or barrier semaphores. Data moves between devices by JAX's collectives and lax.ppermute only.
A program may use at most 128 MiB of HBM per device.

```python
import math
import jax
import jax.numpy as jnp
import numpy as np
from jax import lax

D = 2048
QUERY_HEADS = 32
KEY_VALUE_HEADS = 4
HEAD_SIZE = 128
FF = 768
TOPK = 8
TOK_DEV = 128
EXPERTS = 16
SESSION_COUNT = 4
SESSION_LENGTH = 512
CAP = 96
N_TENSOR = 2


def draw_q_rows(key, part):
    random_key = jax.random.fold_in(key, 1)
    base_rows = jnp.clip(1.7 * jax.random.normal(random_key, (SESSION_COUNT, SESSION_LENGTH, QUERY_HEADS * HEAD_SIZE), jnp.float32), -6.0, 6.0)
    return base_rows.astype(jnp.bfloat16)


def draw_k_rows(key, part):
    random_key = jax.random.fold_in(key, 2)
    base_rows = jnp.clip(1.7 * jax.random.normal(random_key, (SESSION_COUNT, SESSION_LENGTH, KEY_VALUE_HEADS * HEAD_SIZE), jnp.float32), -6.0, 6.0)
    return base_rows.astype(jnp.bfloat16)


def draw_x_rows(key, part):
    random_key = jax.random.fold_in(key, 3)
    row_key = jax.random.fold_in(key, 4)
    column_key = jax.random.fold_in(key, 5)
    spread = 1.15
    base_rows = jnp.clip(jax.random.normal(random_key, (SESSION_COUNT, SESSION_LENGTH, D), jnp.float32), -4.0, 4.0)
    row_scale = jnp.exp(jax.random.uniform(row_key, (SESSION_COUNT, SESSION_LENGTH, 1), jnp.float32, -spread, spread))
    column_scale = jnp.exp(jax.random.uniform(column_key, (1, 1, D), jnp.float32, -spread, spread))
    return (base_rows * row_scale * column_scale).astype(jnp.bfloat16)


def block_scale(key, extent, cuts, least, high):
    loudness = 1.0
    for position, shards_of in cuts:
        draws = jax.random.uniform(jax.random.fold_in(jax.random.fold_in(key, 6), position), (shards_of,), jnp.float32, least / len(cuts), high / len(cuts))
        loudness = loudness * jnp.repeat(jnp.exp(draws), extent[position] // shards_of).reshape((-1,) + (1,) * (len(extent) - 1 - position))
    return loudness


def deal_out(rng, own, number, rows, number_of, top, limit, slope):
    ranking = jax.random.permutation(rng, number_of)
    crowded, common = load_shares(number_of, rows * top, limit, slope, True), load_shares(number_of, rows * top, limit, slope, False)
    places = jnp.arange(number_of)

    def named(sizes, rotation):
        used = int((sizes > 0).sum())
        fixed = max(1, used // 4)
        passed = fixed + (places - fixed + rotation * (used - fixed)) % max(1, number_of - fixed)
        return jnp.zeros((number_of,), jnp.int32).at[ranking[jnp.where(places < fixed, places, passed)]].set(jnp.asarray(sizes, jnp.int32))

    sizes = jnp.where(number % 4 == 0, named(crowded, number // 4), named(common, number - number // 4 - 1))
    mixed = jax.random.permutation(jax.random.fold_in(own, 3), number_of)
    giver, sink = mixed[0:number_of // 2 * 2:2], mixed[1:number_of // 2 * 2:2]
    margin = jnp.minimum(sizes[giver] - 1, limit - sizes[sink]) // 2
    margin = jnp.where((giver == ranking[0]) | (sink == ranking[0]) | (sizes[sink] == 0), 0, jnp.maximum(margin, 0))
    passed = jax.random.randint(jax.random.fold_in(own, 4), (number_of // 2,), 0, 1 << 20) % (margin + 1)
    sizes = sizes.at[giver].add(-passed).at[sink].add(passed)
    members = jnp.searchsorted(jnp.cumsum(sizes), jnp.arange(rows * top), side="right").astype(jnp.int32)
    listing = members.reshape(top, rows).T
    listing = listing[jax.random.permutation(jax.random.fold_in(own, 1), rows)]
    rotation = jax.random.randint(jax.random.fold_in(own, 2), (rows, 1), 0, top)
    return jnp.take_along_axis(listing, (jnp.arange(top)[None, :] + rotation) % top, axis=1)


def load_shares(count, total, limit, skew, full):
    weights = [(1 << 20) // math.isqrt(grade ** skew) + 1 for grade in range(1, count + 1)]
    largest = limit if full else min(limit, max(-(-total // count), total * weights[0] // sum(weights)))
    least = 1 if total - largest >= count - 1 else 0
    holding, rest = [largest] + [least] * (count - 1), total - largest - least * (count - 1)
    while rest > 0:
        free = [i for i in range(1, count) if holding[i] < largest] or [i for i in range(1, count) if holding[i] < limit]
        pool, remaining = sum([weights[i] for i in free]), rest
        for i in free:
            addition = min(limit - holding[i], max(1, remaining * weights[i] // pool), rest)
            holding[i] = holding[i] + addition
            rest = rest - addition
    return np.array(holding)


def scatter_about(rng, shape, scale, most, pieces=(), kind=jnp.bfloat16):
    entries = jax.random.normal(rng, shape, jnp.float32) * scale
    if len(pieces) > 0:
        entries = block_scale(rng, shape, pieces, -0.22, 0.18) * entries
    return jnp.clip(entries, min=-most, max=most).astype(kind)


def setup_inputs(seed: int = 0) -> dict:
    keys = jax.random.split(jax.random.key(seed), 12)
    q_rows = draw_q_rows(jax.random.fold_in(keys[11], 71), 0)
    k_rows = draw_k_rows(jax.random.fold_in(keys[11], 71), 0)
    value_rows = scatter_about(keys[2], (SESSION_COUNT, SESSION_LENGTH, KEY_VALUE_HEADS * HEAD_SIZE), 1.0, 6.0, ((0, 4), (1, 4), (2, 2)))
    x_rows = draw_x_rows(jax.random.fold_in(keys[11], 71), 0)
    out_weight = scatter_about(keys[4], (QUERY_HEADS * HEAD_SIZE, D), (QUERY_HEADS * HEAD_SIZE) ** -0.5, 0.09375, ((0, 2), (1, 4)))
    norm_gain = jnp.clip(1.0 + 0.18 * jax.random.normal(keys[5], (D,), jnp.float32), 0.1, 1.9)
    w_gate = scatter_about(keys[6], (EXPERTS, D, FF), D ** -0.5, 0.125, ((0, 16), (2, 2)))
    w_up = scatter_about(keys[7], (EXPERTS, D, FF), D ** -0.5, 0.125, ((0, 16), (2, 2)))
    w_down = scatter_about(keys[8], (EXPERTS, FF, D), FF ** -0.5, 0.21875, ((0, 16), (1, 2)))
    expert_ids_keys = jax.random.split(jax.random.fold_in(keys[9], 1), SESSION_COUNT * SESSION_LENGTH // TOK_DEV)
    expert_ids_turns = jax.random.permutation(jax.random.fold_in(keys[9], 3), SESSION_COUNT * SESSION_LENGTH // TOK_DEV)
    expert_ids = jax.vmap(lambda own, number: deal_out(jax.random.fold_in(keys[9], 2), own, number, TOK_DEV, EXPERTS, TOPK, CAP, 2))(expert_ids_keys, expert_ids_turns).reshape((SESSION_COUNT, SESSION_LENGTH, TOPK))
    gate_weights = jnp.clip(0.02 + 0.38 * jax.random.uniform(keys[10], (SESSION_COUNT, SESSION_LENGTH, TOPK), jnp.float32) ** block_scale(keys[10], (SESSION_COUNT, SESSION_LENGTH, TOPK), ((0, 4), (1, 4)), -0.2, 0.2), 0.02, 0.4)
    return {"q_rows": q_rows, "k_rows": k_rows, "value_rows": value_rows, "x_rows": x_rows, "out_weight": out_weight, "norm_gain": norm_gain, "w_gate": w_gate, "w_up": w_up, "w_down": w_down, "expert_ids": expert_ids, "gate_weights": gate_weights}


def rounded(value):
    return lax.optimization_barrier(value.astype(jnp.bfloat16)).astype(jnp.float32)

def attend_session(query_session, key_session, value_session):
    group_width = QUERY_HEADS // KEY_VALUE_HEADS
    query_float = query_session.astype(jnp.float32).reshape(SESSION_LENGTH, KEY_VALUE_HEADS, group_width, HEAD_SIZE)
    key_float = key_session.astype(jnp.float32).reshape(SESSION_LENGTH, KEY_VALUE_HEADS, HEAD_SIZE)
    value_float = value_session.astype(jnp.float32).reshape(SESSION_LENGTH, KEY_VALUE_HEADS, HEAD_SIZE)
    scores = jnp.einsum('igrd,jgd->grij', query_float, key_float, precision=lax.Precision.HIGHEST) * (1.0 / math.sqrt(HEAD_SIZE))
    places = jnp.arange(SESSION_LENGTH, dtype=jnp.int32)
    allowed = places[None, :] <= places[:, None]
    scores = jnp.where(allowed, scores, -jnp.inf)
    row_max = lax.optimization_barrier(jnp.max(scores, axis=-1, keepdims=True))
    weights = jnp.where(allowed, jnp.exp(scores - row_max), jnp.float32(0.0))
    totals = lax.optimization_barrier(jnp.sum(weights, axis=-1))
    summed = jnp.einsum('grij,jgd->igrd', rounded(weights), value_float, precision=lax.Precision.HIGHEST)
    result = summed / jnp.transpose(totals, (2, 0, 1))[..., None]
    return result.reshape(SESSION_LENGTH, QUERY_HEADS * HEAD_SIZE).astype(jnp.bfloat16)

def reference(q_rows, k_rows, value_rows, x_rows, out_weight, norm_gain, w_gate, w_up, w_down, expert_ids, gate_weights):
    attn_rows = lax.map(lambda items: attend_session(items[0], items[1], items[2]), (q_rows, k_rows, value_rows))
    all_tokens = SESSION_COUNT * SESSION_LENGTH
    flat_attn = attn_rows.reshape(all_tokens, QUERY_HEADS * HEAD_SIZE)
    head_width = QUERY_HEADS * HEAD_SIZE // N_TENSOR
    projected = jnp.zeros((all_tokens, D), jnp.float32)
    for group_pos in range(N_TENSOR):
        lo_col = group_pos * head_width
        piece = jnp.dot(flat_attn[:, lo_col:lo_col + head_width], out_weight[lo_col:lo_col + head_width], preferred_element_type=jnp.float32)
        projected = projected + rounded(piece)
    mixed = x_rows.reshape(all_tokens, D).astype(jnp.float32) + projected
    inverse = lax.rsqrt(lax.optimization_barrier(jnp.mean(mixed * mixed, axis=1)) + 1e-06)
    normed = (mixed * inverse[:, None] * norm_gain.astype(jnp.float32)[None, :]).astype(jnp.bfloat16)
    blocks = all_tokens // TOK_DEV
    per_block = TOK_DEV * TOPK
    routed = expert_ids.reshape(blocks, per_block)
    member = (routed[:, :, None] == jnp.arange(EXPERTS, dtype=jnp.int32)[None, None, :]).astype(jnp.int32)
    earlier = jnp.cumsum(member, axis=1) - member
    slot_index = lax.optimization_barrier(jnp.sum(earlier * member, axis=2))
    block_index = jnp.arange(blocks, dtype=jnp.int32)[:, None]
    target = (routed * blocks + block_index) * CAP + slot_index
    token_index = block_index * TOK_DEV + jnp.arange(per_block, dtype=jnp.int32)[None, :] // TOPK
    table = jnp.full((EXPERTS * blocks * CAP,), all_tokens, jnp.int32)
    table = table.at[target.reshape(-1)].set(token_index.reshape(-1).astype(jnp.int32)).reshape(EXPERTS, blocks * CAP)
    gate_table = jnp.zeros((EXPERTS * blocks * CAP,), jnp.float32)
    gate_table = gate_table.at[target.reshape(-1)].set(gate_weights.reshape(-1).astype(jnp.float32)).reshape(EXPERTS, blocks * CAP)
    padded = jnp.concatenate([normed, jnp.zeros((1, D), jnp.bfloat16)], axis=0)
    hidden_width = FF // N_TENSOR

    def expert_step(carry, items):
        rows_of, gates_of, gate_w, up_w, down_w = items
        rows = padded[rows_of]
        gate_act = jnp.dot(rows, gate_w, preferred_element_type=jnp.float32)
        up_act = jnp.dot(rows, up_w, preferred_element_type=jnp.float32)
        hidden = (jax.nn.silu(gate_act) * up_act).astype(jnp.bfloat16)
        expert_sum = jnp.zeros((rows.shape[0], D), jnp.float32)
        for group_pos in range(N_TENSOR):
            lo_col = group_pos * hidden_width
            piece = jnp.dot(hidden[:, lo_col:lo_col + hidden_width], down_w[lo_col:lo_col + hidden_width], preferred_element_type=jnp.float32)
            expert_sum = expert_sum + rounded(piece)
        expert_out = expert_sum.astype(jnp.bfloat16).astype(jnp.float32)
        carry = carry.at[rows_of].add(gates_of[:, None] * expert_out)
        return (carry, None)
    starting = jnp.zeros((all_tokens + 1, D), jnp.float32)
    blended, unused = lax.scan(expert_step, starting, (table, gate_table, w_gate, w_up, w_down))
    layer_out = (mixed + blended[:all_tokens]).astype(jnp.bfloat16)
    return layer_out.reshape(SESSION_COUNT, SESSION_LENGTH, D)
```

```python
import functools
import math

import jax
import jax.numpy as jnp
from jax import lax
from jax.experimental import pallas as pl
from jax.experimental.pallas import tpu as pltpu
from jax.sharding import PartitionSpec as P

HEAD_SIZE = 128
TOPK = 8
CHUNKS = 4


def dispatch_plan(
    q_rows,
    k_rows,
    value_rows,
    x_rows,
    out_weight,
    norm_gain,
    w_gate,
    w_up,
    w_down,
    expert_ids,
    gate_weights,
):
    rows_here = q_rows.shape[1]
    kv_heads = k_rows.shape[2] // HEAD_SIZE
    q_heads = q_rows.shape[2] // HEAD_SIZE
    group_width = q_heads // kv_heads
    queries = q_rows[0].reshape(rows_here, kv_heads, group_width, HEAD_SIZE)
    offset = lax.axis_index("seq") * rows_here
    query_pos = offset + jnp.arange(rows_here, dtype=jnp.int32)
    softmax_scale = 1.0 / math.sqrt(HEAD_SIZE)
    tensor_pos = lax.axis_index("tensor")
    tensor_count = lax.axis_size("tensor")
    pieces = (
        lax.all_gather(k_rows, "seq", axis=1, tiled=True),
        lax.all_gather(value_rows, "seq", axis=1, tiled=True),
    )
    running_max = jnp.full((kv_heads, group_width, rows_here), -1e30, jnp.float32)
    block_rows = pieces[0].shape[1]
    key_block = pieces[0][0].reshape(block_rows, kv_heads, HEAD_SIZE)
    value_block = pieces[1][0].reshape(block_rows, kv_heads, HEAD_SIZE)
    scores = (
        jnp.einsum("igrd,jgd->grij", queries, key_block, preferred_element_type=jnp.float32)
        * softmax_scale
    )
    key_pos = jnp.arange(block_rows, dtype=jnp.int32)
    allowed = key_pos[None, :] <= query_pos[:, None]
    scores = jnp.where(allowed, scores, jnp.float32(-1e30))
    new_max = jnp.maximum(running_max, jnp.max(scores, axis=-1))
    weights = jnp.where(allowed, jnp.exp(scores - new_max[..., None]), jnp.float32(0.0))
    running_sum = jnp.sum(weights, axis=-1)
    weighted = jnp.einsum(
        "grij,jgd->grid",
        weights.astype(jnp.bfloat16),
        value_block,
        preferred_element_type=jnp.float32,
    )
    running_max, running_sum, weighted = (new_max, running_sum, weighted)
    attn_rows = (
        (weighted / running_sum[..., None])
        .transpose(2, 0, 1, 3)
        .reshape(rows_here, q_heads * HEAD_SIZE)
        .astype(jnp.bfloat16)
    )
    head_terms = jnp.dot(
        attn_rows,
        lax.all_gather(out_weight, "expert", axis=1, tiled=True),
        preferred_element_type=jnp.float32,
    )
    width = x_rows.shape[2]
    half_width = width // tensor_count
    share_sum = lax.psum_scatter(
        head_terms.astype(jnp.bfloat16), "tensor", scatter_dimension=1, tiled=True
    ).astype(jnp.float32)
    mixed_half = (
        lax.dynamic_slice_in_dim(x_rows[0], tensor_pos * half_width, half_width, 1).astype(
            jnp.float32
        )
        + share_sum
    )
    power = lax.psum(jnp.sum(mixed_half * mixed_half, axis=1), "tensor")
    inverse = lax.rsqrt(power / width + 1e-06)
    normed = (mixed_half * inverse[:, None] * norm_gain[None, :]).astype(jnp.bfloat16)
    seq_count = lax.axis_size("seq")
    group_count = lax.axis_size("expert")
    experts = seq_count * group_count
    capacity = max(2, 3 * rows_here * TOPK // (2 * experts))
    routed = expert_ids[0].reshape(-1)
    assigned = routed.shape[0]
    member = (routed[:, None] == jnp.arange(experts, dtype=jnp.int32)[None, :]).astype(jnp.int32)
    earlier = jnp.cumsum(member, axis=0) - member
    slot_index = jnp.sum(earlier * member, axis=1)
    target = routed * capacity + slot_index
    owner_index = (
        jnp.full((experts * capacity,), assigned, jnp.int32)
        .at[target]
        .set(jnp.arange(assigned, dtype=jnp.int32))
    )
    filled = owner_index < assigned
    source = jnp.minimum(owner_index // TOPK, rows_here - 1)
    outgoing = jnp.where(filled[:, None], normed[source], jnp.zeros((), jnp.bfloat16)).reshape(
        experts, capacity, half_width
    )
    arrived = lax.all_to_all(outgoing, ("seq", "expert"), split_axis=0, concat_axis=0, tiled=True)
    slot_count = arrived.shape[1]
    whole_rows = lax.all_gather(arrived, "tensor", axis=2, tiled=True)
    flat_rows = whole_rows.reshape(-1, whole_rows.shape[2])
    gate_act = jnp.dot(flat_rows, w_gate[0], preferred_element_type=jnp.float32)
    up_act = jnp.dot(flat_rows, w_up[0], preferred_element_type=jnp.float32)
    hidden = (jax.nn.silu(gate_act) * up_act).astype(jnp.bfloat16)
    partial_value = jnp.dot(hidden, w_down[0], preferred_element_type=jnp.float32).reshape(
        arrived.shape[0], slot_count, whole_rows.shape[2]
    )
    returned = lax.all_to_all(
        lax.psum_scatter(
            partial_value.astype(jnp.bfloat16), "tensor", scatter_dimension=2, tiled=True
        ),
        ("seq", "expert"),
        split_axis=0,
        concat_axis=0,
        tiled=True,
    )
    came_back = returned.reshape(experts * capacity, half_width)
    picked = came_back[target].astype(jnp.float32)
    weights_flat = gate_weights[0].reshape(-1)
    blended = jnp.sum((picked * weights_flat[:, None]).reshape(rows_here, TOPK, half_width), axis=1)
    return (mixed_half + blended).astype(jnp.bfloat16)[None]


def bits_of(size):
    return [1 << n for n in range(size.bit_length() - 1)]


def swap(value, axis, bit):
    count = lax.axis_size(axis)
    return lax.ppermute(value, axis, [(i, i ^ bit) for i in range(count)])


def slot_order(bits):
    order = [0]
    for bit in bits:
        order = order + [place ^ bit for place in order]
    return order


def gather_slots(value, axis, bits):
    held = value[None]
    for bit in bits:
        held = jnp.concatenate([held, swap(held, axis, bit)], axis=0)
    return held


def add_rounded(kept, received):
    return (kept.astype(jnp.float32) + received.astype(jnp.float32)).astype(kept.dtype)


def scatter_slots(held, axis, bits):
    for bit in reversed(bits):
        half = held.shape[0] // 2
        held = add_rounded(held[:half], swap(held[half:], axis, bit))
    return held[0]


def expert_kernel(
    order,
    place_ref,
    own_ref,
    other_ref,
    gain_ref,
    gate_ref,
    proj_ref,
    w_gate_ref,
    w_up_ref,
    w_down_ref,
    own_out_ref,
    other_out_ref,
):
    groups, halves, blocks, sessions, rows, piece = own_ref.shape
    half_width = own_out_ref.shape[-1]
    width = half_width * halves
    me, half_me = place_ref[0], place_ref[1]
    my_piece = me * halves + half_me
    per_half = half_width // piece
    count = blocks * sessions * rows
    for which, (in_ref, out_ref) in enumerate(
        ((other_ref, other_out_ref), (own_ref, own_out_ref))
    ):
        power = jnp.zeros((count, 1), jnp.float32)
        pieces = []
        for i in range(groups):
            for k in range(halves):
                tokens = jnp.concatenate(
                    [
                        in_ref[i, k, b, lax.bitwise_xor(me, order[r])]
                        for b in range(blocks)
                        for r in range(sessions)
                    ],
                    axis=0,
                )
                mixed = tokens.astype(jnp.float32)
                power = power + jnp.sum(mixed * mixed, axis=1, keepdims=True)
                pieces.append((i, k, tokens))
        inverse = lax.rsqrt(power * (1.0 / width) + 1e-06)
        gate_act = jnp.zeros((count, w_gate_ref.shape[1]), jnp.float32)
        up_act = jnp.zeros((count, w_up_ref.shape[1]), jnp.float32)
        for i, k, tokens in pieces:
            spot = lax.bitwise_xor(me, order[i]) * halves + lax.bitwise_xor(half_me, k)
            start = pl.multiple_of(spot * piece, piece)
            gain = gain_ref[pl.ds(spot, 1), :]
            normed = (tokens.astype(jnp.float32) * inverse * gain).astype(jnp.bfloat16)
            gate_act += jnp.dot(
                normed, w_gate_ref[pl.ds(start, piece), :], preferred_element_type=jnp.float32
            )
            up_act += jnp.dot(
                normed, w_up_ref[pl.ds(start, piece), :], preferred_element_type=jnp.float32
            )
        hidden = (gate_act / (1.0 + jnp.exp(-gate_act)) * up_act).astype(jnp.bfloat16)
        scale = gate_ref[1 - which]
        for k in range(halves):
            half_at = lax.bitwise_xor(half_me, k)
            start = pl.multiple_of(half_at * half_width, half_width)
            result = scale * jnp.dot(
                hidden,
                w_down_ref[:, pl.ds(start, half_width)],
                preferred_element_type=jnp.float32,
            )
            for b in range(blocks):
                part = result[b * sessions * rows : (b + 1) * sessions * rows]
                if which == 1 and b == 0:
                    proj = proj_ref[...].reshape(sessions * rows, piece)
                    columns = []
                    for n in range(per_half):
                        here = (my_piece == half_at * per_half + n).astype(jnp.float32)
                        columns.append(part[:, n * piece : (n + 1) * piece] + proj * here)
                    part = jnp.concatenate(columns, axis=1)
                part = part.astype(jnp.bfloat16)
                for r in range(sessions):
                    out_ref[r, k, b] = part[r * rows : (r + 1) * rows]


def dense_plan(
    q_rows,
    k_rows,
    value_rows,
    x_rows,
    out_weight,
    norm_gain,
    w_gate,
    w_up,
    w_down,
    expert_ids,
    gate_weights,
):
    rows_here = q_rows.shape[1]
    width = x_rows.shape[2]
    seq_count, group_count = lax.axis_size("seq"), lax.axis_size("expert")
    tensor_count = lax.axis_size("tensor")
    experts = seq_count * group_count
    seq_pos, group_pos = lax.axis_index("seq"), lax.axis_index("expert")
    tensor_pos = lax.axis_index("tensor")
    seq_bits, group_bits = bits_of(seq_count), bits_of(group_count)
    tensor_bits = bits_of(tensor_count)
    half_width = width // tensor_count
    piece = width // (group_count * tensor_count)
    near, far = seq_bits[:1], seq_bits[1:]

    kv_width = k_rows.shape[2]
    kv_all = lax.all_gather(
        jnp.concatenate([k_rows[0], value_rows[0]], axis=1), "seq", axis=0, tiled=True
    )

    x_slots = []
    for r in range(group_count):
        start = ((group_pos ^ r) * tensor_count + tensor_pos) * piece
        columns = lax.dynamic_slice_in_dim(x_rows[0], start, piece, 1)
        x_slots.append(swap(columns, "expert", r) if r else columns)
    gain_slots = gather_slots(norm_gain, "tensor", tensor_bits)
    gain = jnp.take(
        gain_slots,
        jnp.array(slot_order(tensor_bits), jnp.int32) ^ tensor_pos,
        axis=0,
    ).reshape(width // piece, piece)

    named = expert_ids[0][:, :, None] == jnp.arange(experts, dtype=jnp.int32)[None, None, :]
    table = jnp.sum(jnp.where(named, gate_weights[0][:, :, None], 0.0), axis=1).T
    table = lax.all_to_all(
        table, ("seq", "expert"), split_axis=0, concat_axis=0, tiled=True
    ).reshape(seq_count, group_count, rows_here)
    table = jnp.take(table, jnp.arange(seq_count, dtype=jnp.int32) ^ seq_pos, axis=0)

    kv_heads = kv_width // HEAD_SIZE
    q_heads = q_rows.shape[2] // HEAD_SIZE
    group_width = q_heads // kv_heads
    queries = q_rows[0].reshape(rows_here, kv_heads, group_width, HEAD_SIZE)
    query_pos = seq_pos * rows_here + jnp.arange(rows_here, dtype=jnp.int32)
    block_rows = kv_all.shape[0]
    key_block = kv_all[:, :kv_width].reshape(block_rows, kv_heads, HEAD_SIZE)
    value_block = kv_all[:, kv_width:].reshape(block_rows, kv_heads, HEAD_SIZE)
    scores = jnp.einsum(
        "igrd,jgd->grij", queries, key_block, preferred_element_type=jnp.float32
    ) * (1.0 / math.sqrt(HEAD_SIZE))
    allowed = jnp.arange(block_rows, dtype=jnp.int32)[None, :] <= query_pos[:, None]
    scores = jnp.where(allowed, scores, jnp.float32(-1e30))
    weights = jnp.where(
        allowed, jnp.exp(scores - jnp.max(scores, axis=-1, keepdims=True)), jnp.float32(0.0)
    )
    totals = jnp.sum(weights, axis=-1)
    weighted = jnp.einsum(
        "grij,jgd->grid",
        weights.astype(jnp.bfloat16),
        value_block,
        preferred_element_type=jnp.float32,
    )
    attn_rows = (
        (weighted / totals[..., None])
        .transpose(2, 0, 1, 3)
        .reshape(rows_here, q_heads * HEAD_SIZE)
        .astype(jnp.bfloat16)
    )

    paths = (group_bits, group_bits[::-1])
    depth = attn_rows.shape[1] // len(paths)
    gathered = []
    for n, path in enumerate(paths):
        held = gather_slots(attn_rows[:, n * depth : (n + 1) * depth], "expert", path)
        order = slot_order(path)
        gathered.append(
            jnp.concatenate([held[order.index(r)] for r in range(group_count)], axis=0)
        )

    def projected(k):
        columns = lax.dynamic_slice_in_dim(out_weight, (tensor_pos ^ k) * piece, piece, 1)
        return sum(
            jnp.dot(
                held, columns[n * depth : (n + 1) * depth], preferred_element_type=jnp.float32
            )
            for n, held in enumerate(gathered)
        )

    proj = projected(0)
    for k in range(1, tensor_count):
        away = projected(k).astype(jnp.bfloat16)
        proj = proj + swap(away, "tensor", k).astype(jnp.float32)
    proj = proj.reshape(group_count, rows_here, piece)
    mixed = (jnp.stack(x_slots).astype(jnp.float32) + proj).astype(jnp.bfloat16)
    by_session = jnp.take(
        mixed, jnp.arange(group_count, dtype=jnp.int32) ^ group_pos, axis=0
    )

    rows = rows_here // CHUNKS
    place = jnp.stack([group_pos, tensor_pos]).astype(jnp.int32)
    finished = []
    for c in range(CHUNKS):
        path = paths[c % len(paths)]
        order = slot_order(path)
        held = by_session[:, c * rows : (c + 1) * rows]
        held = gather_slots(held, "seq", far)
        held = gather_slots(held, "tensor", tensor_bits)
        held = gather_slots(held, "expert", path)
        other = swap(held, "seq", near[0])
        places = jnp.array(order, jnp.int32) ^ group_pos
        gates = jnp.take(table[:, :, c * rows : (c + 1) * rows], places, axis=1)
        far_order = slot_order(far)
        gates = jnp.stack(
            [
                jnp.stack([gates[f ^ near_bit] for f in far_order])
                for near_bit in (0, near[0])
            ]
        ).reshape(2, -1, 1)
        own_proj = jnp.stack([proj[r, c * rows : (c + 1) * rows] for r in order])
        out_type = jax.ShapeDtypeStruct(
            (group_count, tensor_count, len(far_order), rows, half_width), jnp.bfloat16
        )
        kernel = pl.pallas_call(
            functools.partial(expert_kernel, tuple(order)),
            out_shape=(out_type, out_type),
            in_specs=[pl.BlockSpec(memory_space=pltpu.SMEM)]
            + [pl.BlockSpec(memory_space=pltpu.VMEM)] * 8,
            out_specs=(pl.BlockSpec(memory_space=pltpu.VMEM),) * 2,
            name=f"experts_{c}",
        )
        own_out, other_out = kernel(
            place, held, other, gain, gates, own_proj, w_gate[0], w_up[0], w_down[0]
        )
        total = add_rounded(own_out, swap(other_out, "seq", near[0]))
        total = scatter_slots(total, "expert", path)
        total = scatter_slots(total, "tensor", tensor_bits)
        finished.append(scatter_slots(total, "seq", far))
    x_half = lax.dynamic_slice_in_dim(x_rows[0], tensor_pos * half_width, half_width, 1)
    summed = jnp.concatenate(finished, axis=0).astype(jnp.float32)
    return (x_half.astype(jnp.float32) + summed).astype(jnp.bfloat16)[None]


def per_device(*arrays):
    rows_here = arrays[0].shape[1]
    counts = [lax.axis_size(axis) for axis in ("seq", "expert", "tensor")]
    experts = counts[0] * counts[1]
    capacity = max(2, 3 * rows_here * TOPK // (2 * experts))
    dense = experts * rows_here <= 2 * experts * capacity
    regular = all(count > 1 and count & (count - 1) == 0 for count in counts)
    if dense and regular and rows_here % (16 * CHUNKS) == 0:
        return dense_plan(*arrays)
    return dispatch_plan(*arrays)


def solution(mesh):
    return jax.shard_map(
        per_device,
        mesh=mesh,
        in_specs=(
            P("expert", "seq", "tensor"),
            P("expert", "seq", "tensor"),
            P("expert", "seq", "tensor"),
            P("expert", "seq", None),
            P("tensor", "expert"),
            P("tensor"),
            P(("seq", "expert"), None, "tensor"),
            P(("seq", "expert"), None, "tensor"),
            P(("seq", "expert"), "tensor", None),
            P("expert", "seq", None),
            P("expert", "seq", None),
        ),
        out_specs=P("expert", "seq", "tensor"),
        check_vma=False,
    )
```

```python
import functools
import math

import jax
import jax.numpy as jnp
from jax import lax
from jax.experimental import pallas as pl
from jax.experimental.pallas import tpu as pltpu
from jax.sharding import PartitionSpec as P


HEAD_SIZE = 128
TOPK = 8
CHUNKS = 2
KERNEL_BYTES = 24 << 20


def dispatch_plan(
    q_rows,
    k_rows,
    value_rows,
    x_rows,
    out_weight,
    norm_gain,
    w_gate,
    w_up,
    w_down,
    expert_ids,
    gate_weights,
):
    rows_here = q_rows.shape[1]
    kv_heads = k_rows.shape[2] // HEAD_SIZE
    q_heads = q_rows.shape[2] // HEAD_SIZE
    group_width = q_heads // kv_heads
    queries = q_rows[0].reshape(rows_here, kv_heads, group_width, HEAD_SIZE)
    offset = lax.axis_index("seq") * rows_here
    query_pos = offset + jnp.arange(rows_here, dtype=jnp.int32)
    softmax_scale = 1.0 / math.sqrt(HEAD_SIZE)
    tensor_pos = lax.axis_index("tensor")
    tensor_count = lax.axis_size("tensor")
    pieces = (
        lax.all_gather(k_rows, "seq", axis=1, tiled=True),
        lax.all_gather(value_rows, "seq", axis=1, tiled=True),
    )
    running_max = jnp.full((kv_heads, group_width, rows_here), -1e30, jnp.float32)
    block_rows = pieces[0].shape[1]
    key_block = pieces[0][0].reshape(block_rows, kv_heads, HEAD_SIZE)
    value_block = pieces[1][0].reshape(block_rows, kv_heads, HEAD_SIZE)
    scores = (
        jnp.einsum("igrd,jgd->grij", queries, key_block, preferred_element_type=jnp.float32)
        * softmax_scale
    )
    key_pos = jnp.arange(block_rows, dtype=jnp.int32)
    allowed = key_pos[None, :] <= query_pos[:, None]
    scores = jnp.where(allowed, scores, jnp.float32(-1e30))
    new_max = jnp.maximum(running_max, jnp.max(scores, axis=-1))
    weights = jnp.where(allowed, jnp.exp(scores - new_max[..., None]), jnp.float32(0.0))
    running_sum = jnp.sum(weights, axis=-1)
    weighted = jnp.einsum(
        "grij,jgd->grid",
        weights.astype(jnp.bfloat16),
        value_block,
        preferred_element_type=jnp.float32,
    )
    running_max, running_sum, weighted = (new_max, running_sum, weighted)
    attn_rows = (
        (weighted / running_sum[..., None])
        .transpose(2, 0, 1, 3)
        .reshape(rows_here, q_heads * HEAD_SIZE)
        .astype(jnp.bfloat16)
    )
    head_terms = jnp.dot(
        attn_rows,
        lax.all_gather(out_weight, "expert", axis=1, tiled=True),
        preferred_element_type=jnp.float32,
    )
    width = x_rows.shape[2]
    half_width = width // tensor_count
    share_sum = lax.psum_scatter(
        head_terms.astype(jnp.bfloat16), "tensor", scatter_dimension=1, tiled=True
    ).astype(jnp.float32)
    mixed_half = (
        lax.dynamic_slice_in_dim(x_rows[0], tensor_pos * half_width, half_width, 1).astype(
            jnp.float32
        )
        + share_sum
    )
    power = lax.psum(jnp.sum(mixed_half * mixed_half, axis=1), "tensor")
    inverse = lax.rsqrt(power / width + 1e-06)
    normed = (mixed_half * inverse[:, None] * norm_gain[None, :]).astype(jnp.bfloat16)
    seq_count = lax.axis_size("seq")
    group_count = lax.axis_size("expert")
    experts = seq_count * group_count
    capacity = max(2, 3 * rows_here * TOPK // (2 * experts))
    routed = expert_ids[0].reshape(-1)
    assigned = routed.shape[0]
    member = (routed[:, None] == jnp.arange(experts, dtype=jnp.int32)[None, :]).astype(jnp.int32)
    earlier = jnp.cumsum(member, axis=0) - member
    slot_index = jnp.sum(earlier * member, axis=1)
    target = routed * capacity + slot_index
    owner_index = (
        jnp.full((experts * capacity,), assigned, jnp.int32)
        .at[target]
        .set(jnp.arange(assigned, dtype=jnp.int32))
    )
    filled = owner_index < assigned
    source = jnp.minimum(owner_index // TOPK, rows_here - 1)
    outgoing = jnp.where(filled[:, None], normed[source], jnp.zeros((), jnp.bfloat16)).reshape(
        experts, capacity, half_width
    )
    arrived = lax.all_to_all(outgoing, ("seq", "expert"), split_axis=0, concat_axis=0, tiled=True)
    slot_count = arrived.shape[1]
    whole_rows = lax.all_gather(arrived, "tensor", axis=2, tiled=True)
    flat_rows = whole_rows.reshape(-1, whole_rows.shape[2])
    gate_act = jnp.dot(flat_rows, w_gate[0], preferred_element_type=jnp.float32)
    up_act = jnp.dot(flat_rows, w_up[0], preferred_element_type=jnp.float32)
    hidden = (jax.nn.silu(gate_act) * up_act).astype(jnp.bfloat16)
    partial_value = jnp.dot(hidden, w_down[0], preferred_element_type=jnp.float32).reshape(
        arrived.shape[0], slot_count, whole_rows.shape[2]
    )
    returned = lax.all_to_all(
        lax.psum_scatter(
            partial_value.astype(jnp.bfloat16), "tensor", scatter_dimension=2, tiled=True
        ),
        ("seq", "expert"),
        split_axis=0,
        concat_axis=0,
        tiled=True,
    )
    came_back = returned.reshape(experts * capacity, half_width)
    picked = came_back[target].astype(jnp.float32)
    weights_flat = gate_weights[0].reshape(-1)
    blended = jnp.sum((picked * weights_flat[:, None]).reshape(rows_here, TOPK, half_width), axis=1)
    return (mixed_half + blended).astype(jnp.bfloat16)[None]


def bits_of(size):
    return [1 << n for n in range(size.bit_length() - 1)]


def swap(value, axis, bit):
    count = lax.axis_size(axis)
    return lax.ppermute(value, axis, [(i, i ^ bit) for i in range(count)])


def slot_order(bits):
    order = [0]
    for bit in bits:
        order = order + [place ^ bit for place in order]
    return order


def gather_slots(value, axis, bits):
    held = value[None]
    for bit in bits:
        held = jnp.concatenate([held, swap(held, axis, bit)], axis=0)
    return held


def add_rounded(kept, received):
    return (kept.astype(jnp.float32) + received.astype(jnp.float32)).astype(kept.dtype)


def scatter_slots(held, axis, bits):
    for bit in reversed(bits):
        half = held.shape[0] // 2
        held = add_rounded(held[:half], swap(held[half:], axis, bit))
    return held[0]


def expert_kernel(order, slots, near, start_row, has_received, *refs):
    refs = list(refs)
    place_ref, first_ref, second_ref, gain_ref, table_ref = refs[:5]
    del refs[:5]
    proj_ref = None if near else refs.pop(0)
    received_ref = refs.pop(0) if has_received else None
    w_in_ref, w_out_ref, out_ref, normed_ref = refs
    half_groups, halves, blocks, sessions, rows, piece = first_ref.shape
    half_width = out_ref.shape[-1]
    width = half_width * halves
    hidden_width = w_out_ref.shape[0]
    me, half_me, seq_me = place_ref[0], place_ref[1], place_ref[2]
    per_half = half_width // piece
    count = len(slots) * rows * blocks

    power = jnp.zeros((count, 1), jnp.float32)
    pieces = []
    for i in range(2 * half_groups):
        in_ref = first_ref if i < half_groups else second_ref
        for k in range(halves):
            tokens = jnp.concatenate(
                [
                    in_ref[i % half_groups, k, b, lax.bitwise_xor(me, order[r])]
                    for b in range(blocks)
                    for r in slots
                ],
                axis=0,
            )
            mixed = tokens.astype(jnp.float32)
            power = power + jnp.sum(mixed * mixed, axis=1, keepdims=True)
            pieces.append((i, k, tokens))
    inverse = lax.rsqrt(power * (1.0 / width) + 1e-06)
    for i, k, tokens in pieces:
        spot = lax.bitwise_xor(me, order[i]) * halves + lax.bitwise_xor(half_me, k)
        gain = gain_ref[pl.ds(spot, 1), :]
        normed_ref[:, pl.ds(pl.multiple_of(spot * piece, piece), piece)] = (
            tokens.astype(jnp.float32) * inverse * gain
        ).astype(jnp.bfloat16)
    both = jnp.dot(normed_ref[...], w_in_ref[...], preferred_element_type=jnp.float32)
    gate_act, up_act = both[:, :hidden_width], both[:, hidden_width:]
    hidden = (gate_act / (1.0 + jnp.exp(-gate_act)) * up_act).astype(jnp.bfloat16)

    diagonal = lax.broadcasted_iota(jnp.int32, (rows, rows), 0) == lax.broadcasted_iota(
        jnp.int32, (rows, rows), 1
    )
    scales = []
    for b in range(blocks):
        for r in slots:
            source = lax.bitwise_xor(seq_me, 2 * b + near) * sessions
            source = source + lax.bitwise_xor(me, order[r])
            line = table_ref[pl.ds(source, 1), :][:, start_row : start_row + rows]
            scales.append(
                jnp.sum(jnp.where(diagonal, line, 0.0), axis=1, keepdims=True)
            )
    scale = jnp.concatenate(scales, axis=0)
    for half in range(halves):
        k = lax.bitwise_xor(half_me, half)
        result = scale * jnp.dot(
            hidden,
            w_out_ref[:, half * half_width : (half + 1) * half_width],
            preferred_element_type=jnp.float32,
        )
        at = 0
        for b in range(blocks):
            for n, r in enumerate(slots):
                part = result[at : at + rows]
                at += rows
                if proj_ref is not None and b == 0:
                    proj = proj_ref[order[r], start_row : start_row + rows]
                    columns = []
                    for m in range(per_half):
                        mine = me * halves + half_me == half * per_half + m
                        columns.append(
                            part[:, m * piece : (m + 1) * piece]
                            + proj * mine.astype(jnp.float32)
                        )
                    part = jnp.concatenate(columns, axis=1)
                if received_ref is not None:
                    part = part + received_ref[n, k, b].astype(jnp.float32)
                out_ref[n, k, b] = part.astype(jnp.bfloat16)


def dense_plan(
    q_rows,
    k_rows,
    value_rows,
    x_rows,
    out_weight,
    norm_gain,
    w_gate,
    w_up,
    w_down,
    expert_ids,
    gate_weights,
):
    rows_here = q_rows.shape[1]
    width = x_rows.shape[2]
    seq_count, group_count = lax.axis_size("seq"), lax.axis_size("expert")
    tensor_count = lax.axis_size("tensor")
    experts = seq_count * group_count
    seq_pos, group_pos = lax.axis_index("seq"), lax.axis_index("expert")
    tensor_pos = lax.axis_index("tensor")
    seq_bits, group_bits = bits_of(seq_count), bits_of(group_count)
    tensor_bits = bits_of(tensor_count)
    half_width = width // tensor_count
    piece = width // (group_count * tensor_count)
    near, far = seq_bits[:1], seq_bits[1:]

    kv_width = k_rows.shape[2]
    kv_bits = far + near
    kv_all = gather_slots(
        jnp.concatenate([k_rows[0], value_rows[0]], axis=1), "seq", kv_bits
    ).reshape(seq_count * rows_here, 2 * kv_width)
    key_pos = (seq_pos ^ jnp.array(slot_order(kv_bits), jnp.int32))[:, None] * rows_here
    key_pos = (key_pos + jnp.arange(rows_here, dtype=jnp.int32)[None, :]).reshape(-1)

    x_slots = []
    for r in range(group_count):
        start = ((group_pos ^ r) * tensor_count + tensor_pos) * piece
        columns = lax.dynamic_slice_in_dim(x_rows[0], start, piece, 1)
        x_slots.append(swap(columns, "expert", r) if r else columns)
    gain_slots = gather_slots(norm_gain, "tensor", tensor_bits)
    gain = jnp.take(
        gain_slots,
        jnp.array(slot_order(tensor_bits), jnp.int32) ^ tensor_pos,
        axis=0,
    ).reshape(width // piece, piece)

    named = expert_ids[0][:, :, None] == jnp.arange(experts, dtype=jnp.int32)[None, None, :]
    table = jnp.sum(jnp.where(named, gate_weights[0][:, :, None], 0.0), axis=1).T
    table = lax.all_to_all(table, ("seq", "expert"), split_axis=0, concat_axis=0, tiled=True)
    w_in = jnp.concatenate([w_gate[0], w_up[0]], axis=1)
    kv_all, table, gain, w_in, *x_slots = lax.optimization_barrier(
        (kv_all, table, gain, w_in, *x_slots)
    )

    kv_heads = kv_width // HEAD_SIZE
    q_heads = q_rows.shape[2] // HEAD_SIZE
    group_width = q_heads // kv_heads
    queries = q_rows[0].reshape(rows_here, kv_heads, group_width, HEAD_SIZE)
    query_pos = seq_pos * rows_here + jnp.arange(rows_here, dtype=jnp.int32)
    block_rows = kv_all.shape[0]
    key_block = kv_all[:, :kv_width].reshape(block_rows, kv_heads, HEAD_SIZE)
    value_block = kv_all[:, kv_width:].reshape(block_rows, kv_heads, HEAD_SIZE)
    scores = jnp.einsum(
        "igrd,jgd->grij", queries, key_block, preferred_element_type=jnp.float32
    ) * (1.0 / math.sqrt(HEAD_SIZE))
    allowed = key_pos[None, :] <= query_pos[:, None]
    scores = jnp.where(allowed, scores, jnp.float32(-1e30))
    weights = jnp.where(
        allowed, jnp.exp(scores - jnp.max(scores, axis=-1, keepdims=True)), jnp.float32(0.0)
    )
    totals = jnp.sum(weights, axis=-1)
    weighted = jnp.einsum(
        "grij,jgd->grid",
        weights.astype(jnp.bfloat16),
        value_block,
        preferred_element_type=jnp.float32,
    )
    attn_rows = (
        (weighted / totals[..., None])
        .transpose(2, 0, 1, 3)
        .reshape(rows_here, q_heads * HEAD_SIZE)
        .astype(jnp.bfloat16)
    )

    paths = (group_bits, group_bits[::-1])
    depth = attn_rows.shape[1] // len(paths)
    gathered = []
    for n, path in enumerate(paths):
        held = [attn_rows[:, n * depth : (n + 1) * depth]]
        for bit in path:
            held = held + [swap(value, "expert", bit) for value in held]
        order = slot_order(path)
        gathered.append(
            jnp.concatenate([held[order.index(r)] for r in range(group_count)], axis=0)
        )

    def projected(k):
        columns = lax.dynamic_slice_in_dim(out_weight, (tensor_pos ^ k) * piece, piece, 1)
        return sum(
            jnp.dot(
                held, columns[n * depth : (n + 1) * depth], preferred_element_type=jnp.float32
            )
            for n, held in enumerate(gathered)
        )

    proj = projected(0)
    for k in range(1, tensor_count):
        away = projected(k).astype(jnp.bfloat16)
        proj = proj + swap(away, "tensor", k).astype(jnp.float32)
    proj = proj.reshape(group_count, rows_here, piece)
    mixed = (jnp.stack(x_slots).astype(jnp.float32) + proj).astype(jnp.bfloat16)
    by_session = jnp.take(
        mixed, jnp.arange(group_count, dtype=jnp.int32) ^ group_pos, axis=0
    )

    rows = rows_here // CHUNKS
    place = jnp.stack([group_pos, tensor_pos, seq_pos]).astype(jnp.int32)
    half_groups = group_count // 2
    near_bit = near[0]
    chunks = []
    for c in range(CHUNKS):
        path = paths[c % len(paths)]
        held = by_session[:, c * rows : (c + 1) * rows]
        held = gather_slots(held, "seq", far)
        held = gather_slots(held, "tensor", tensor_bits)
        first = gather_slots(held, "expert", path[:-1])
        second = swap(first, "expert", path[-1])
        parts = ((first, second), tuple(swap(v, "seq", near_bit) for v in (first, second)))
        chunks.append((c, path, parts))

    def experts_on(place, c, path, parts, slots, core, received):
        operands = [place, *parts[core], gain, table]
        if not core:
            operands.append(proj)
        if received is not None:
            operands.append(received)
        operands += [w_in, w_down[0]]
        blocks = seq_count // 2
        return pl.pallas_call(
            functools.partial(
                expert_kernel,
                tuple(slot_order(path)),
                tuple(slots),
                core,
                c * rows,
                received is not None,
            ),
            out_shape=jax.ShapeDtypeStruct(
                (len(slots), tensor_count, blocks, rows, half_width), jnp.bfloat16
            ),
            in_specs=[pl.BlockSpec(memory_space=pltpu.SMEM)]
            + [pl.BlockSpec(memory_space=pltpu.VMEM)] * (len(operands) - 1),
            out_specs=pl.BlockSpec(memory_space=pltpu.VMEM),
            scratch_shapes=[pltpu.VMEM((len(slots) * blocks * rows, width), jnp.bfloat16)],
            compiler_params=pltpu.CompilerParams(vmem_limit_bytes=KERNEL_BYTES),
        )(*operands)

    sent, kept = range(half_groups, group_count), range(half_groups)
    totals = []
    for slots in (sent, kept):
        away, outs = [], []
        for chunk in chunks:
            away.append(experts_on(place, *chunk, slots, 1, None))
        away = [swap(value, "seq", near_bit) for value in away]
        for chunk, got in zip(chunks, away):
            outs.append(experts_on(place, *chunk, slots, 0, got))
        place = lax.optimization_barrier((place, *outs))[0]
        totals.append(outs)
    finished = []
    for (c, path, _), away, held in zip(chunks, *totals):
        arrived = swap(away, "expert", path[-1])
        held = add_rounded(held, arrived)
        held = scatter_slots(held, "expert", path[:-1])
        held = scatter_slots(held, "tensor", tensor_bits)
        finished.append(scatter_slots(held, "seq", far))
    x_half = lax.dynamic_slice_in_dim(x_rows[0], tensor_pos * half_width, half_width, 1)
    summed = jnp.concatenate(finished, axis=0).astype(jnp.float32)
    return (x_half.astype(jnp.float32) + summed).astype(jnp.bfloat16)[None]


def per_device(*arrays):
    rows_here = arrays[0].shape[1]
    counts = [lax.axis_size(axis) for axis in ("seq", "expert", "tensor")]
    experts = counts[0] * counts[1]
    capacity = max(2, 3 * rows_here * TOPK // (2 * experts))
    dense = experts * rows_here <= 2 * experts * capacity
    regular = all(count > 1 and count & (count - 1) == 0 for count in counts)
    if dense and regular and rows_here % (16 * CHUNKS) == 0:
        return dense_plan(*arrays)
    return dispatch_plan(*arrays)


def solution(mesh):
    return jax.shard_map(
        per_device,
        mesh=mesh,
        in_specs=(
            P("expert", "seq", "tensor"),
            P("expert", "seq", "tensor"),
            P("expert", "seq", "tensor"),
            P("expert", "seq", None),
            P("tensor", "expert"),
            P("tensor"),
            P(("seq", "expert"), None, "tensor"),
            P(("seq", "expert"), None, "tensor"),
            P(("seq", "expert"), "tensor", None),
            P("expert", "seq", None),
            P("expert", "seq", None),
        ),
        out_specs=P("expert", "seq", "tensor"),
        check_vma=False,
    )
```

```python
import functools
import math

import jax
import jax.numpy as jnp
from jax import lax
from jax.experimental import pallas as pl
from jax.experimental.pallas import tpu as pltpu
from jax.sharding import PartitionSpec as P


HEAD_SIZE = 128
TOPK = 8
CHUNKS = 4
KERNEL_BYTES = 20 << 20


def dispatch_plan(
    q_rows,
    k_rows,
    value_rows,
    x_rows,
    out_weight,
    norm_gain,
    w_gate,
    w_up,
    w_down,
    expert_ids,
    gate_weights,
):
    rows_here = q_rows.shape[1]
    kv_heads = k_rows.shape[2] // HEAD_SIZE
    q_heads = q_rows.shape[2] // HEAD_SIZE
    group_width = q_heads // kv_heads
    queries = q_rows[0].reshape(rows_here, kv_heads, group_width, HEAD_SIZE)
    offset = lax.axis_index("seq") * rows_here
    query_pos = offset + jnp.arange(rows_here, dtype=jnp.int32)
    softmax_scale = 1.0 / math.sqrt(HEAD_SIZE)
    tensor_pos = lax.axis_index("tensor")
    tensor_count = lax.axis_size("tensor")
    pieces = (
        lax.all_gather(k_rows, "seq", axis=1, tiled=True),
        lax.all_gather(value_rows, "seq", axis=1, tiled=True),
    )
    running_max = jnp.full((kv_heads, group_width, rows_here), -1e30, jnp.float32)
    block_rows = pieces[0].shape[1]
    key_block = pieces[0][0].reshape(block_rows, kv_heads, HEAD_SIZE)
    value_block = pieces[1][0].reshape(block_rows, kv_heads, HEAD_SIZE)
    scores = (
        jnp.einsum("igrd,jgd->grij", queries, key_block, preferred_element_type=jnp.float32)
        * softmax_scale
    )
    key_pos = jnp.arange(block_rows, dtype=jnp.int32)
    allowed = key_pos[None, :] <= query_pos[:, None]
    scores = jnp.where(allowed, scores, jnp.float32(-1e30))
    new_max = jnp.maximum(running_max, jnp.max(scores, axis=-1))
    weights = jnp.where(allowed, jnp.exp(scores - new_max[..., None]), jnp.float32(0.0))
    running_sum = jnp.sum(weights, axis=-1)
    weighted = jnp.einsum(
        "grij,jgd->grid",
        weights.astype(jnp.bfloat16),
        value_block,
        preferred_element_type=jnp.float32,
    )
    running_max, running_sum, weighted = (new_max, running_sum, weighted)
    attn_rows = (
        (weighted / running_sum[..., None])
        .transpose(2, 0, 1, 3)
        .reshape(rows_here, q_heads * HEAD_SIZE)
        .astype(jnp.bfloat16)
    )
    head_terms = jnp.dot(
        attn_rows,
        lax.all_gather(out_weight, "expert", axis=1, tiled=True),
        preferred_element_type=jnp.float32,
    )
    width = x_rows.shape[2]
    half_width = width // tensor_count
    share_sum = lax.psum_scatter(
        head_terms.astype(jnp.bfloat16), "tensor", scatter_dimension=1, tiled=True
    ).astype(jnp.float32)
    mixed_half = (
        lax.dynamic_slice_in_dim(x_rows[0], tensor_pos * half_width, half_width, 1).astype(
            jnp.float32
        )
        + share_sum
    )
    power = lax.psum(jnp.sum(mixed_half * mixed_half, axis=1), "tensor")
    inverse = lax.rsqrt(power / width + 1e-06)
    normed = (mixed_half * inverse[:, None] * norm_gain[None, :]).astype(jnp.bfloat16)
    seq_count = lax.axis_size("seq")
    group_count = lax.axis_size("expert")
    experts = seq_count * group_count
    capacity = max(2, 3 * rows_here * TOPK // (2 * experts))
    routed = expert_ids[0].reshape(-1)
    assigned = routed.shape[0]
    member = (routed[:, None] == jnp.arange(experts, dtype=jnp.int32)[None, :]).astype(jnp.int32)
    earlier = jnp.cumsum(member, axis=0) - member
    slot_index = jnp.sum(earlier * member, axis=1)
    target = routed * capacity + slot_index
    owner_index = (
        jnp.full((experts * capacity,), assigned, jnp.int32)
        .at[target]
        .set(jnp.arange(assigned, dtype=jnp.int32))
    )
    filled = owner_index < assigned
    source = jnp.minimum(owner_index // TOPK, rows_here - 1)
    outgoing = jnp.where(filled[:, None], normed[source], jnp.zeros((), jnp.bfloat16)).reshape(
        experts, capacity, half_width
    )
    arrived = lax.all_to_all(outgoing, ("seq", "expert"), split_axis=0, concat_axis=0, tiled=True)
    slot_count = arrived.shape[1]
    whole_rows = lax.all_gather(arrived, "tensor", axis=2, tiled=True)
    flat_rows = whole_rows.reshape(-1, whole_rows.shape[2])
    gate_act = jnp.dot(flat_rows, w_gate[0], preferred_element_type=jnp.float32)
    up_act = jnp.dot(flat_rows, w_up[0], preferred_element_type=jnp.float32)
    hidden = (jax.nn.silu(gate_act) * up_act).astype(jnp.bfloat16)
    partial_value = jnp.dot(hidden, w_down[0], preferred_element_type=jnp.float32).reshape(
        arrived.shape[0], slot_count, whole_rows.shape[2]
    )
    returned = lax.all_to_all(
        lax.psum_scatter(
            partial_value.astype(jnp.bfloat16), "tensor", scatter_dimension=2, tiled=True
        ),
        ("seq", "expert"),
        split_axis=0,
        concat_axis=0,
        tiled=True,
    )
    came_back = returned.reshape(experts * capacity, half_width)
    picked = came_back[target].astype(jnp.float32)
    weights_flat = gate_weights[0].reshape(-1)
    blended = jnp.sum((picked * weights_flat[:, None]).reshape(rows_here, TOPK, half_width), axis=1)
    return (mixed_half + blended).astype(jnp.bfloat16)[None]


def bits_of(size):
    return [1 << n for n in range(size.bit_length() - 1)]


def swap(value, axis, bit):
    count = lax.axis_size(axis)
    return lax.ppermute(value, axis, [(i, i ^ bit) for i in range(count)])


def slot_order(bits):
    order = [0]
    for bit in bits:
        order = order + [place ^ bit for place in order]
    return order


def gather_slots(value, axis, bits):
    held = value[None]
    for bit in bits:
        held = jnp.concatenate([held, swap(held, axis, bit)], axis=0)
    return held


def gather_parts(value, axis, bits):
    held = [value]
    for bit in bits:
        arrived = []
        for part in held:
            arrived.append(swap(part, axis, bit))
        held = held + arrived
    return held


def total(terms):
    if len(terms) == 1:
        return terms[0]
    return sum(term.astype(jnp.float32) for term in terms).astype(terms[0].dtype)


def return_parts(parts, axis, bits):
    held = [[part] for part in parts]
    for bit in reversed(bits):
        half = len(held) // 2
        arrived = [None] * half
        for i in reversed(range(half)):
            arrived[i] = swap(total(held[half + i]), axis, bit)
        held = [terms + [extra] for terms, extra in zip(held, arrived)]
    return held[0]


def return_rows(terms, axis, bits):
    for bit in reversed(bits):
        half = terms[0].shape[0] // 2
        arrived = swap(total([term[half:] for term in terms]), axis, bit)
        terms = [term[:half] for term in terms] + [arrived]
    return [term[0] for term in terms]


def expert_kernel(order, near, start_row, *refs):
    groups = len(order)
    refs = list(refs)
    place_ref, gain_ref, table_ref, w_in_ref, w_out_ref = refs[:5]
    in_refs, refs = refs[5 : 5 + groups], refs[5 + groups :]
    proj_ref, received_ref = (None, None) if near else (refs.pop(0), refs.pop(0))
    normed_ref = refs.pop()
    halves, blocks, sessions, rows, piece = in_refs[0].shape
    half_width = refs[0].shape[-1]
    width = half_width * halves
    hidden_width = w_out_ref.shape[0]
    me, half_me, seq_me = place_ref[0], place_ref[1], place_ref[2]
    per_half = half_width // piece
    count = groups * rows * blocks

    power = jnp.zeros((count, 1), jnp.float32)
    pieces = []
    for i, in_ref in enumerate(in_refs):
        for k in range(halves):
            tokens = jnp.concatenate(
                [
                    in_ref[k, b, lax.bitwise_xor(me, order[r])]
                    for b in range(blocks)
                    for r in range(groups)
                ],
                axis=0,
            )
            mixed = tokens.astype(jnp.float32)
            power = power + jnp.sum(mixed * mixed, axis=1, keepdims=True)
            pieces.append((i, k, tokens))
    inverse = lax.rsqrt(power * (1.0 / width) + 1e-06)
    for i, k, tokens in pieces:
        spot = lax.bitwise_xor(me, order[i]) * halves + lax.bitwise_xor(half_me, k)
        gain = gain_ref[pl.ds(spot, 1), :]
        normed_ref[:, pl.ds(pl.multiple_of(spot * piece, piece), piece)] = (
            tokens.astype(jnp.float32) * inverse * gain
        ).astype(jnp.bfloat16)
    both = jnp.dot(normed_ref[...], w_in_ref[...], preferred_element_type=jnp.float32)
    gate_act, up_act = both[:, :hidden_width], both[:, hidden_width:]
    hidden = (gate_act / (1.0 + jnp.exp(-gate_act)) * up_act).astype(jnp.bfloat16)

    diagonal = lax.broadcasted_iota(jnp.int32, (rows, rows), 0) == lax.broadcasted_iota(
        jnp.int32, (rows, rows), 1
    )
    scales = []
    for b in range(blocks):
        for r in range(groups):
            source = lax.bitwise_xor(seq_me, 2 * b + near) * sessions
            source = source + lax.bitwise_xor(me, order[r])
            line = table_ref[pl.ds(source, 1), :][:, start_row : start_row + rows]
            scales.append(
                jnp.sum(jnp.where(diagonal, line, 0.0), axis=1, keepdims=True)
            )
    scale = jnp.concatenate(scales, axis=0)
    for half in range(halves):
        k = lax.bitwise_xor(half_me, half)
        result = scale * jnp.dot(
            hidden,
            w_out_ref[:, half * half_width : (half + 1) * half_width],
            preferred_element_type=jnp.float32,
        )
        at = 0
        for b in range(blocks):
            for r in range(groups):
                part = result[at : at + rows]
                at += rows
                if proj_ref is not None and b == 0:
                    proj = proj_ref[order[r], start_row : start_row + rows]
                    columns = []
                    for m in range(per_half):
                        mine = me * halves + half_me == half * per_half + m
                        columns.append(
                            part[:, m * piece : (m + 1) * piece]
                            + proj * mine.astype(jnp.float32)
                        )
                    part = jnp.concatenate(columns, axis=1)
                if received_ref is not None:
                    part = part + received_ref[r, k, b].astype(jnp.float32)
                part = part.astype(jnp.bfloat16)
                if near:
                    refs[0][r, k, b] = part
                else:
                    refs[r][k, b] = part


def dense_plan(
    q_rows,
    k_rows,
    value_rows,
    x_rows,
    out_weight,
    norm_gain,
    w_gate,
    w_up,
    w_down,
    expert_ids,
    gate_weights,
):
    rows_here = q_rows.shape[1]
    width = x_rows.shape[2]
    seq_count, group_count = lax.axis_size("seq"), lax.axis_size("expert")
    tensor_count = lax.axis_size("tensor")
    experts = seq_count * group_count
    seq_pos, group_pos = lax.axis_index("seq"), lax.axis_index("expert")
    tensor_pos = lax.axis_index("tensor")
    seq_bits, group_bits = bits_of(seq_count), bits_of(group_count)
    tensor_bits = bits_of(tensor_count)
    half_width = width // tensor_count
    piece = width // (group_count * tensor_count)
    near, far = seq_bits[:1], seq_bits[1:]

    kv_width = k_rows.shape[2]
    kv_bits = far + near
    kv_all = jnp.concatenate(
        gather_parts(jnp.concatenate([k_rows[0], value_rows[0]], axis=1), "seq", kv_bits),
        axis=0,
    )
    key_pos = (seq_pos ^ jnp.array(slot_order(kv_bits), jnp.int32))[:, None] * rows_here
    key_pos = (key_pos + jnp.arange(rows_here, dtype=jnp.int32)[None, :]).reshape(-1)

    x_slots = []
    for r in range(group_count):
        start = ((group_pos ^ r) * tensor_count + tensor_pos) * piece
        columns = lax.dynamic_slice_in_dim(x_rows[0], start, piece, 1)
        x_slots.append(swap(columns, "expert", r) if r else columns)
    kv_all, *x_slots = lax.optimization_barrier((kv_all, *x_slots))

    kv_heads = kv_width // HEAD_SIZE
    q_heads = q_rows.shape[2] // HEAD_SIZE
    group_width = q_heads // kv_heads
    queries = q_rows[0].reshape(rows_here, kv_heads, group_width, HEAD_SIZE)
    query_pos = seq_pos * rows_here + jnp.arange(rows_here, dtype=jnp.int32)
    block_rows = kv_all.shape[0]
    key_block = kv_all[:, :kv_width].reshape(block_rows, kv_heads, HEAD_SIZE)
    value_block = kv_all[:, kv_width:].reshape(block_rows, kv_heads, HEAD_SIZE)
    scores = jnp.einsum(
        "igrd,jgd->grij", queries, key_block, preferred_element_type=jnp.float32
    ) * (1.0 / math.sqrt(HEAD_SIZE))
    allowed = key_pos[None, :] <= query_pos[:, None]
    scores = jnp.where(allowed, scores, jnp.float32(-1e30))
    weights = jnp.where(
        allowed, jnp.exp(scores - jnp.max(scores, axis=-1, keepdims=True)), jnp.float32(0.0)
    )
    totals = jnp.sum(weights, axis=-1)
    weighted = jnp.einsum(
        "grij,jgd->grid",
        weights.astype(jnp.bfloat16),
        value_block,
        preferred_element_type=jnp.float32,
    )
    attn_rows = (
        (weighted / totals[..., None])
        .transpose(2, 0, 1, 3)
        .reshape(rows_here, q_heads * HEAD_SIZE)
        .astype(jnp.bfloat16)
    )

    attn_rows, expert_ids, gate_weights, norm_gain, w_gate, w_up = lax.optimization_barrier(
        (attn_rows, expert_ids, gate_weights, norm_gain, w_gate, w_up)
    )
    gain_slots = gather_slots(norm_gain, "tensor", tensor_bits)
    gain_at = jnp.array(slot_order(tensor_bits), jnp.int32) ^ tensor_pos
    gain = gain_slots.at[gain_at].get(mode="promise_in_bounds").reshape(width // piece, piece)
    named = expert_ids[0][:, :, None] == jnp.arange(experts, dtype=jnp.int32)[None, None, :]
    table = jnp.sum(jnp.where(named, gate_weights[0][:, :, None], 0.0), axis=1).T
    table = lax.all_to_all(table, ("seq", "expert"), split_axis=0, concat_axis=0, tiled=True)
    w_in = jnp.concatenate([w_gate[0], w_up[0]], axis=1)

    paths = (group_bits, group_bits[::-1])
    depth = attn_rows.shape[1] // len(paths)
    gathered = []
    for n, path in enumerate(paths):
        held = gather_parts(attn_rows[:, n * depth : (n + 1) * depth], "expert", path)
        order = slot_order(path)
        gathered.append(
            jnp.concatenate([held[order.index(r)] for r in range(group_count)], axis=0)
        )

    def projected(k):
        columns = lax.dynamic_slice_in_dim(out_weight, (tensor_pos ^ k) * piece, piece, 1)
        return sum(
            jnp.dot(
                held, columns[n * depth : (n + 1) * depth], preferred_element_type=jnp.float32
            )
            for n, held in enumerate(gathered)
        )

    proj = projected(0)
    for k in range(1, tensor_count):
        away = projected(k).astype(jnp.bfloat16)
        proj = proj + swap(away, "tensor", k).astype(jnp.float32)
    proj = proj.reshape(group_count, rows_here, piece)
    mixed = (jnp.stack(x_slots).astype(jnp.float32) + proj).astype(jnp.bfloat16)
    session_at = jnp.arange(group_count, dtype=jnp.int32) ^ group_pos
    by_session = mixed.at[session_at].get(mode="promise_in_bounds")
    by_session, gain, table, w_in = lax.optimization_barrier((by_session, gain, table, w_in))

    rows = rows_here // CHUNKS
    blocks = seq_count // 2
    place = jnp.stack([group_pos, tensor_pos, seq_pos]).astype(jnp.int32)
    chunks = []
    for c in range(CHUNKS):
        path = paths[c % len(paths)]
        held = by_session[:, c * rows : (c + 1) * rows]
        held = gather_slots(held, "seq", far)
        held = gather_slots(held, "tensor", tensor_bits)
        own = gather_parts(held, "expert", path)
        other = []
        for part in own:
            other.append(swap(part, "seq", near[0]))
        chunks.append((c, path, own, other))

    def experts_on(c, path, parts, received):
        order = tuple(slot_order(path))
        operands = [place, gain, table, w_in, w_down[0], *parts]
        shape = (tensor_count, blocks, rows, half_width)
        if received is None:
            shapes = [jax.ShapeDtypeStruct((group_count, *shape), jnp.bfloat16)]
        else:
            operands += [proj, received]
            shapes = [jax.ShapeDtypeStruct(shape, jnp.bfloat16)] * group_count
        near_order = near[0] if received is None else 0
        return pl.pallas_call(
            functools.partial(expert_kernel, order, near_order, c * rows),
            out_shape=shapes,
            in_specs=[pl.BlockSpec(memory_space=pltpu.SMEM)]
            + [pl.BlockSpec(memory_space=pltpu.VMEM)] * (len(operands) - 1),
            out_specs=[pl.BlockSpec(memory_space=pltpu.VMEM)] * len(shapes),
            scratch_shapes=[pltpu.VMEM((group_count * blocks * rows, width), jnp.bfloat16)],
            compiler_params=pltpu.CompilerParams(vmem_limit_bytes=KERNEL_BYTES),
        )(*operands)

    finished = []
    for c, path, own, other in chunks:
        (away,) = experts_on(c, path, other, None)
        away = swap(away, "seq", near[0])
        parts = experts_on(c, path, own, away)
        terms = return_parts(parts, "expert", path)
        terms = return_rows(terms, "tensor", tensor_bits)
        terms = return_rows(terms, "seq", far)
        finished.append(sum(term.astype(jnp.float32) for term in terms))
    x_half = lax.dynamic_slice_in_dim(x_rows[0], tensor_pos * half_width, half_width, 1)
    summed = jnp.concatenate(finished, axis=0)
    return (x_half.astype(jnp.float32) + summed).astype(jnp.bfloat16)[None]


def per_device(*arrays):
    rows_here = arrays[0].shape[1]
    counts = [lax.axis_size(axis) for axis in ("seq", "expert", "tensor")]
    experts = counts[0] * counts[1]
    capacity = max(2, 3 * rows_here * TOPK // (2 * experts))
    dense = experts * rows_here <= 2 * experts * capacity
    regular = all(count > 1 and count & (count - 1) == 0 for count in counts)
    if dense and regular and rows_here % (16 * CHUNKS) == 0:
        return dense_plan(*arrays)
    return dispatch_plan(*arrays)


def solution(mesh):
    return jax.shard_map(
        per_device,
        mesh=mesh,
        in_specs=(
            P("expert", "seq", "tensor"),
            P("expert", "seq", "tensor"),
            P("expert", "seq", "tensor"),
            P("expert", "seq", None),
            P("tensor", "expert"),
            P("tensor"),
            P(("seq", "expert"), None, "tensor"),
            P(("seq", "expert"), None, "tensor"),
            P(("seq", "expert"), "tensor", None),
            P("expert", "seq", None),
            P("expert", "seq", None),
        ),
        out_specs=P("expert", "seq", "tensor"),
        check_vma=False,
    )
```

```python
import functools
import math

import jax
import jax.numpy as jnp
from jax import lax
from jax.experimental import pallas as pl
from jax.experimental.pallas import tpu as pltpu
from jax.sharding import PartitionSpec as P


HEAD_SIZE = 128
TOPK = 8
CHUNKS = 4
KERNEL_BYTES = 6 << 20


def dispatch_plan(
    q_rows,
    k_rows,
    value_rows,
    x_rows,
    out_weight,
    norm_gain,
    w_gate,
    w_up,
    w_down,
    expert_ids,
    gate_weights,
):
    rows_here = q_rows.shape[1]
    kv_heads = k_rows.shape[2] // HEAD_SIZE
    q_heads = q_rows.shape[2] // HEAD_SIZE
    group_width = q_heads // kv_heads
    queries = q_rows[0].reshape(rows_here, kv_heads, group_width, HEAD_SIZE)
    offset = lax.axis_index("seq") * rows_here
    query_pos = offset + jnp.arange(rows_here, dtype=jnp.int32)
    softmax_scale = 1.0 / math.sqrt(HEAD_SIZE)
    tensor_pos = lax.axis_index("tensor")
    tensor_count = lax.axis_size("tensor")
    pieces = (
        lax.all_gather(k_rows, "seq", axis=1, tiled=True),
        lax.all_gather(value_rows, "seq", axis=1, tiled=True),
    )
    running_max = jnp.full((kv_heads, group_width, rows_here), -1e30, jnp.float32)
    block_rows = pieces[0].shape[1]
    key_block = pieces[0][0].reshape(block_rows, kv_heads, HEAD_SIZE)
    value_block = pieces[1][0].reshape(block_rows, kv_heads, HEAD_SIZE)
    scores = (
        jnp.einsum("igrd,jgd->grij", queries, key_block, preferred_element_type=jnp.float32)
        * softmax_scale
    )
    key_pos = jnp.arange(block_rows, dtype=jnp.int32)
    allowed = key_pos[None, :] <= query_pos[:, None]
    scores = jnp.where(allowed, scores, jnp.float32(-1e30))
    new_max = jnp.maximum(running_max, jnp.max(scores, axis=-1))
    weights = jnp.where(allowed, jnp.exp(scores - new_max[..., None]), jnp.float32(0.0))
    running_sum = jnp.sum(weights, axis=-1)
    weighted = jnp.einsum(
        "grij,jgd->grid",
        weights.astype(jnp.bfloat16),
        value_block,
        preferred_element_type=jnp.float32,
    )
    running_max, running_sum, weighted = (new_max, running_sum, weighted)
    attn_rows = (
        (weighted / running_sum[..., None])
        .transpose(2, 0, 1, 3)
        .reshape(rows_here, q_heads * HEAD_SIZE)
        .astype(jnp.bfloat16)
    )
    head_terms = jnp.dot(
        attn_rows,
        lax.all_gather(out_weight, "expert", axis=1, tiled=True),
        preferred_element_type=jnp.float32,
    )
    width = x_rows.shape[2]
    half_width = width // tensor_count
    share_sum = lax.psum_scatter(
        head_terms.astype(jnp.bfloat16), "tensor", scatter_dimension=1, tiled=True
    ).astype(jnp.float32)
    mixed_half = (
        lax.dynamic_slice_in_dim(x_rows[0], tensor_pos * half_width, half_width, 1).astype(
            jnp.float32
        )
        + share_sum
    )
    power = lax.psum(jnp.sum(mixed_half * mixed_half, axis=1), "tensor")
    inverse = lax.rsqrt(power / width + 1e-06)
    normed = (mixed_half * inverse[:, None] * norm_gain[None, :]).astype(jnp.bfloat16)
    seq_count = lax.axis_size("seq")
    group_count = lax.axis_size("expert")
    experts = seq_count * group_count
    capacity = max(2, 3 * rows_here * TOPK // (2 * experts))
    routed = expert_ids[0].reshape(-1)
    assigned = routed.shape[0]
    member = (routed[:, None] == jnp.arange(experts, dtype=jnp.int32)[None, :]).astype(jnp.int32)
    earlier = jnp.cumsum(member, axis=0) - member
    slot_index = jnp.sum(earlier * member, axis=1)
    target = routed * capacity + slot_index
    owner_index = (
        jnp.full((experts * capacity,), assigned, jnp.int32)
        .at[target]
        .set(jnp.arange(assigned, dtype=jnp.int32))
    )
    filled = owner_index < assigned
    source = jnp.minimum(owner_index // TOPK, rows_here - 1)
    outgoing = jnp.where(filled[:, None], normed[source], jnp.zeros((), jnp.bfloat16)).reshape(
        experts, capacity, half_width
    )
    arrived = lax.all_to_all(outgoing, ("seq", "expert"), split_axis=0, concat_axis=0, tiled=True)
    slot_count = arrived.shape[1]
    whole_rows = lax.all_gather(arrived, "tensor", axis=2, tiled=True)
    flat_rows = whole_rows.reshape(-1, whole_rows.shape[2])
    gate_act = jnp.dot(flat_rows, w_gate[0], preferred_element_type=jnp.float32)
    up_act = jnp.dot(flat_rows, w_up[0], preferred_element_type=jnp.float32)
    hidden = (jax.nn.silu(gate_act) * up_act).astype(jnp.bfloat16)
    partial_value = jnp.dot(hidden, w_down[0], preferred_element_type=jnp.float32).reshape(
        arrived.shape[0], slot_count, whole_rows.shape[2]
    )
    returned = lax.all_to_all(
        lax.psum_scatter(
            partial_value.astype(jnp.bfloat16), "tensor", scatter_dimension=2, tiled=True
        ),
        ("seq", "expert"),
        split_axis=0,
        concat_axis=0,
        tiled=True,
    )
    came_back = returned.reshape(experts * capacity, half_width)
    picked = came_back[target].astype(jnp.float32)
    weights_flat = gate_weights[0].reshape(-1)
    blended = jnp.sum((picked * weights_flat[:, None]).reshape(rows_here, TOPK, half_width), axis=1)
    return (mixed_half + blended).astype(jnp.bfloat16)[None]


def bits_of(size):
    return [1 << n for n in range(size.bit_length() - 1)]


def swap(value, axis, bit):
    count = lax.axis_size(axis)
    return lax.ppermute(value, axis, [(i, i ^ bit) for i in range(count)])


def slot_order(bits):
    order = [0]
    for bit in bits:
        order = order + [place ^ bit for place in order]
    return order


def gather_slots(value, axis, bits):
    held = value[None]
    for bit in bits:
        held = jnp.concatenate([held, swap(held, axis, bit)], axis=0)
    return held


def gather_parts(value, axis, bits):
    held = [value]
    for bit in bits:
        arrived = []
        for part in held:
            arrived.append(swap(part, axis, bit))
        held = held + arrived
    return held


def total(terms):
    if len(terms) == 1:
        return terms[0]
    return sum(term.astype(jnp.float32) for term in terms).astype(terms[0].dtype)


def return_parts(parts, axis, bits):
    held = [[part] for part in parts]
    for bit in reversed(bits):
        half = len(held) // 2
        arrived = [None] * half
        for i in reversed(range(half)):
            arrived[i] = swap(total(held[half + i]), axis, bit)
        held = [terms + [extra] for terms, extra in zip(held, arrived)]
    return held[0]


def return_rows(terms, axis, bits):
    for bit in reversed(bits):
        half = terms[0].shape[0] // 2
        arrived = swap(total([term[half:] for term in terms]), axis, bit)
        terms = [term[:half] for term in terms] + [arrived]
    return [term[0] for term in terms]


def expert_kernel(order, near, start_row, *refs):
    groups = len(order)
    refs = list(refs)
    place_ref, gain_ref, table_ref, w_in_ref, w_out_ref = refs[:5]
    in_refs, refs = refs[5 : 5 + groups], refs[5 + groups :]
    proj_ref, received_ref = (None, None) if near else (refs.pop(0), refs.pop(0))
    normed_ref = refs.pop()
    halves, blocks, sessions, rows, piece = in_refs[0].shape
    half_width = refs[0].shape[-1]
    width = half_width * halves
    hidden_width = w_out_ref.shape[0]
    me, half_me, seq_me = place_ref[0], place_ref[1], place_ref[2]
    per_half = half_width // piece
    count = groups * rows * blocks

    power = jnp.zeros((count, 1), jnp.float32)
    pieces = []
    for i, in_ref in enumerate(in_refs):
        for k in range(halves):
            tokens = jnp.concatenate(
                [
                    in_ref[k, b, lax.bitwise_xor(me, order[r])]
                    for b in range(blocks)
                    for r in range(groups)
                ],
                axis=0,
            )
            mixed = tokens.astype(jnp.float32)
            power = power + jnp.sum(mixed * mixed, axis=1, keepdims=True)
            pieces.append((i, k, tokens))
    inverse = lax.rsqrt(power * (1.0 / width) + 1e-06)
    for i, k, tokens in pieces:
        spot = lax.bitwise_xor(me, order[i]) * halves + lax.bitwise_xor(half_me, k)
        gain = gain_ref[pl.ds(spot, 1), :]
        normed_ref[:, pl.ds(pl.multiple_of(spot * piece, piece), piece)] = (
            tokens.astype(jnp.float32) * inverse * gain
        ).astype(jnp.bfloat16)
    both = jnp.dot(normed_ref[...], w_in_ref[...], preferred_element_type=jnp.float32)
    gate_act, up_act = both[:, :hidden_width], both[:, hidden_width:]
    hidden = (gate_act / (1.0 + jnp.exp(-gate_act)) * up_act).astype(jnp.bfloat16)

    diagonal = lax.broadcasted_iota(jnp.int32, (rows, rows), 0) == lax.broadcasted_iota(
        jnp.int32, (rows, rows), 1
    )
    scales = []
    for b in range(blocks):
        for r in range(groups):
            source = lax.bitwise_xor(seq_me, 2 * b + near) * sessions
            source = source + lax.bitwise_xor(me, order[r])
            line = table_ref[pl.ds(source, 1), :][:, start_row : start_row + rows]
            scales.append(
                jnp.sum(jnp.where(diagonal, line, 0.0), axis=1, keepdims=True)
            )
    scale = jnp.concatenate(scales, axis=0)
    for half in range(halves):
        k = lax.bitwise_xor(half_me, half)
        result = scale * jnp.dot(
            hidden,
            w_out_ref[:, half * half_width : (half + 1) * half_width],
            preferred_element_type=jnp.float32,
        )
        at = 0
        for b in range(blocks):
            for r in range(groups):
                part = result[at : at + rows]
                at += rows
                if proj_ref is not None and b == 0:
                    proj = proj_ref[order[r], start_row : start_row + rows]
                    columns = []
                    for m in range(per_half):
                        mine = me * halves + half_me == half * per_half + m
                        columns.append(
                            part[:, m * piece : (m + 1) * piece]
                            + proj * mine.astype(jnp.float32)
                        )
                    part = jnp.concatenate(columns, axis=1)
                if received_ref is not None:
                    part = part + received_ref[r, k, b].astype(jnp.float32)
                part = part.astype(jnp.bfloat16)
                if near:
                    refs[0][r, k, b] = part
                else:
                    refs[r][k, b] = part


def attention_kernel(head, order, place_ref, q_ref, *refs):
    slots = len(order)
    k_refs, v_refs, out_ref = refs[:slots], refs[slots : 2 * slots], refs[-1]
    rows = q_ref.shape[0]
    columns = slice(head * HEAD_SIZE, (head + 1) * HEAD_SIZE)
    keys = jnp.concatenate([ref[:, columns] for ref in k_refs], axis=0)
    values = jnp.concatenate([ref[:, columns] for ref in v_refs], axis=0)
    down = lax.broadcasted_iota(jnp.int32, (rows, rows), 0)
    across = lax.broadcasted_iota(jnp.int32, (rows, rows), 1)
    seq_me = place_ref[2]
    allowed = jnp.concatenate(
        [
            (lax.bitwise_xor(seq_me, place) - seq_me) * rows + across <= down
            for place in order
        ],
        axis=1,
    )
    for n in range(out_ref.shape[1] // HEAD_SIZE):
        start = head * out_ref.shape[1] + n * HEAD_SIZE
        scores = lax.dot_general(
            q_ref[:, start : start + HEAD_SIZE],
            keys,
            (((1,), (1,)), ((), ())),
            preferred_element_type=jnp.float32,
        ) * (1.0 / math.sqrt(HEAD_SIZE))
        scores = jnp.where(allowed, scores, jnp.float32(-1e30))
        weights = jnp.exp(scores - jnp.max(scores, axis=1, keepdims=True))
        weights = jnp.where(allowed, weights, jnp.float32(0.0))
        mixed = jnp.dot(
            weights.astype(jnp.bfloat16), values, preferred_element_type=jnp.float32
        )
        mixed = mixed / jnp.sum(weights, axis=1, keepdims=True)
        out_ref[:, n * HEAD_SIZE : (n + 1) * HEAD_SIZE] = mixed.astype(jnp.bfloat16)


def project_kernel(away, place_ref, w_ref, *refs):
    out_ref, joined_ref = refs[-2:]
    sessions, rows, piece = out_ref.shape
    depth = refs[0].shape[1]
    for n, ref in enumerate(refs[:-2]):
        half, r = divmod(n, sessions)
        joined_ref[r * rows : (r + 1) * rows, half * depth : (half + 1) * depth] = ref[...]
    start = pl.multiple_of(lax.bitwise_xor(place_ref[1], away) * piece, piece)
    result = jnp.dot(
        joined_ref[...], w_ref[:, pl.ds(start, piece)], preferred_element_type=jnp.float32
    )
    out_ref[...] = result.reshape(sessions, rows, piece).astype(out_ref.dtype)


def mix_kernel(sessions, place_ref, *refs):
    x_refs, refs = refs[:sessions], refs[sessions:]
    terms, (proj_ref, *chunk_refs) = refs[: -1 - CHUNKS], refs[-1 - CHUNKS :]
    rows = chunk_refs[0].shape[1]
    me = place_ref[0]
    for r in range(sessions):
        proj = sum(ref[r].astype(jnp.float32) for ref in terms)
        proj_ref[r] = proj
        mixed = (x_refs[r][...].astype(jnp.float32) + proj).astype(jnp.bfloat16)
        for c, chunk_ref in enumerate(chunk_refs):
            chunk_ref[lax.bitwise_xor(me, r)] = mixed[c * rows : (c + 1) * rows]


def local_kernel(kernel, outs, operands, scratch=(), limit=12 << 20):
    return pl.pallas_call(
        kernel,
        out_shape=outs,
        in_specs=[pl.BlockSpec(memory_space=pltpu.SMEM)]
        + [pl.BlockSpec(memory_space=pltpu.VMEM)] * (len(operands) - 1),
        out_specs=[pl.BlockSpec(memory_space=pltpu.VMEM)] * len(outs),
        scratch_shapes=scratch,
        compiler_params=pltpu.CompilerParams(vmem_limit_bytes=limit),
    )(*operands)


def dense_plan(
    q_rows,
    k_rows,
    value_rows,
    x_rows,
    out_weight,
    norm_gain,
    w_gate,
    w_up,
    w_down,
    expert_ids,
    gate_weights,
):
    rows_here = q_rows.shape[1]
    width = x_rows.shape[2]
    seq_count, group_count = lax.axis_size("seq"), lax.axis_size("expert")
    tensor_count = lax.axis_size("tensor")
    experts = seq_count * group_count
    seq_pos, group_pos = lax.axis_index("seq"), lax.axis_index("expert")
    tensor_pos = lax.axis_index("tensor")
    seq_bits, group_bits = bits_of(seq_count), bits_of(group_count)
    tensor_bits = bits_of(tensor_count)
    half_width = width // tensor_count
    piece = width // (group_count * tensor_count)
    near, far = seq_bits[:1], seq_bits[1:]

    place = jnp.stack([group_pos, tensor_pos, seq_pos]).astype(jnp.int32)

    kv_bits = far + near
    keys = gather_parts(k_rows[0], "seq", kv_bits)
    values = gather_parts(value_rows[0], "seq", kv_bits)

    x_slots = []
    for r in range(group_count):
        start = ((group_pos ^ r) * tensor_count + tensor_pos) * piece
        columns = lax.dynamic_slice_in_dim(x_rows[0], start, piece, 1)
        x_slots.append(swap(columns, "expert", r) if r else columns)

    kv_heads = k_rows.shape[2] // HEAD_SIZE
    depth = q_rows.shape[2] // kv_heads
    attended = []
    for head in range(kv_heads):
        attended += local_kernel(
            functools.partial(attention_kernel, head, tuple(slot_order(kv_bits))),
            [jax.ShapeDtypeStruct((rows_here, depth), jnp.bfloat16)],
            [place, q_rows[0], *keys, *values],
        )

    expert_ids, gate_weights, norm_gain, w_gate, w_up, _ = lax.optimization_barrier(
        (expert_ids, gate_weights, norm_gain, w_gate, w_up, attended[0])
    )
    gain_slots = gather_slots(norm_gain, "tensor", tensor_bits)
    gain_at = jnp.array(slot_order(tensor_bits), jnp.int32) ^ tensor_pos
    gain = gain_slots.at[gain_at].get(mode="promise_in_bounds").reshape(width // piece, piece)
    named = expert_ids[0][:, :, None] == jnp.arange(experts, dtype=jnp.int32)[None, None, :]
    table = jnp.sum(jnp.where(named, gate_weights[0][:, :, None], 0.0), axis=1).T
    table = lax.all_to_all(table, ("seq", "expert"), split_axis=0, concat_axis=0, tiled=True)
    w_in = jnp.concatenate([w_gate[0], w_up[0]], axis=1)

    paths = (group_bits, group_bits[::-1])
    gathered = []
    for n, rows_of in enumerate(attended):
        path = paths[n % len(paths)]
        held = gather_parts(rows_of, "expert", path)
        order = slot_order(path)
        gathered += [held[order.index(r)] for r in range(group_count)]

    def projected(k, kind):
        shape = (group_count, rows_here, piece)
        return local_kernel(
            functools.partial(project_kernel, k),
            [jax.ShapeDtypeStruct(shape, kind)],
            [place, out_weight, *gathered],
            [pltpu.VMEM((group_count * rows_here, out_weight.shape[0]), jnp.bfloat16)],
        )[0]

    terms = []
    for k in range(1, tensor_count):
        away = projected(k, jnp.bfloat16)
        terms.append(swap(away, "tensor", k))
    terms.append(projected(0, jnp.float32))
    rows = rows_here // CHUNKS
    part = jax.ShapeDtypeStruct((group_count, rows, piece), jnp.bfloat16)
    proj, *by_session = local_kernel(
        functools.partial(mix_kernel, group_count),
        [jax.ShapeDtypeStruct((group_count, rows_here, piece), jnp.float32)] + [part] * CHUNKS,
        [place, *x_slots, *terms],
    )
    gain, table, w_in, *by_session = lax.optimization_barrier(
        (gain, table, w_in, *by_session)
    )

    blocks = seq_count // 2
    chunks = []
    for c in range(CHUNKS):
        path = paths[c % len(paths)]
        held = by_session[c]
        held = gather_slots(held, "seq", far)
        held = gather_slots(held, "tensor", tensor_bits)
        own = gather_parts(held, "expert", path)
        other = []
        for part in own:
            other.append(swap(part, "seq", near[0]))
        chunks.append((c, path, own, other))

    def experts_on(c, path, parts, received):
        order = tuple(slot_order(path))
        operands = [place, gain, table, w_in, w_down[0], *parts]
        shape = (tensor_count, blocks, rows, half_width)
        if received is None:
            shapes = [jax.ShapeDtypeStruct((group_count, *shape), jnp.bfloat16)]
        else:
            operands += [proj, received]
            shapes = [jax.ShapeDtypeStruct(shape, jnp.bfloat16)] * group_count
        near_order = near[0] if received is None else 0
        return local_kernel(
            functools.partial(expert_kernel, order, near_order, c * rows),
            shapes,
            operands,
            [pltpu.VMEM((group_count * blocks * rows, width), jnp.bfloat16)],
            KERNEL_BYTES,
        )

    finished = []
    for c, path, own, other in chunks:
        (away,) = experts_on(c, path, other, None)
        away = swap(away, "seq", near[0])
        parts = experts_on(c, path, own, away)
        terms = return_parts(parts, "expert", path)
        terms = return_rows(terms, "tensor", tensor_bits)
        terms = return_rows(terms, "seq", far)
        finished.append(sum(term.astype(jnp.float32) for term in terms))
    x_half = lax.dynamic_slice_in_dim(x_rows[0], tensor_pos * half_width, half_width, 1)
    summed = jnp.concatenate(finished, axis=0)
    return (x_half.astype(jnp.float32) + summed).astype(jnp.bfloat16)[None]


def per_device(*arrays):
    rows_here = arrays[0].shape[1]
    counts = [lax.axis_size(axis) for axis in ("seq", "expert", "tensor")]
    experts = counts[0] * counts[1]
    capacity = max(2, 3 * rows_here * TOPK // (2 * experts))
    dense = experts * rows_here <= 2 * experts * capacity
    regular = all(count > 1 and count & (count - 1) == 0 for count in counts)
    if dense and regular and rows_here % (16 * CHUNKS) == 0:
        return dense_plan(*arrays)
    return dispatch_plan(*arrays)


def solution(mesh):
    return jax.shard_map(
        per_device,
        mesh=mesh,
        in_specs=(
            P("expert", "seq", "tensor"),
            P("expert", "seq", "tensor"),
            P("expert", "seq", "tensor"),
            P("expert", "seq", None),
            P("tensor", "expert"),
            P("tensor"),
            P(("seq", "expert"), None, "tensor"),
            P(("seq", "expert"), None, "tensor"),
            P(("seq", "expert"), "tensor", None),
            P("expert", "seq", None),
            P("expert", "seq", None),
        ),
        out_specs=P("expert", "seq", "tensor"),
        check_vma=False,
    )
```

```python
import functools
import math

import jax
import jax.numpy as jnp
from jax import lax
from jax.experimental import pallas as pl
from jax.experimental.pallas import tpu as pltpu
from jax.sharding import PartitionSpec as P


HEAD_SIZE = 128
TOPK = 8
LANES = 128
CHUNKS = 4
KERNEL_BYTES = 6 << 20


def dispatch_plan(
    q_rows,
    k_rows,
    value_rows,
    x_rows,
    out_weight,
    norm_gain,
    w_gate,
    w_up,
    w_down,
    expert_ids,
    gate_weights,
):
    rows_here = q_rows.shape[1]
    kv_heads = k_rows.shape[2] // HEAD_SIZE
    q_heads = q_rows.shape[2] // HEAD_SIZE
    group_width = q_heads // kv_heads
    queries = q_rows[0].reshape(rows_here, kv_heads, group_width, HEAD_SIZE)
    offset = lax.axis_index("seq") * rows_here
    query_pos = offset + jnp.arange(rows_here, dtype=jnp.int32)
    softmax_scale = 1.0 / math.sqrt(HEAD_SIZE)
    tensor_pos = lax.axis_index("tensor")
    tensor_count = lax.axis_size("tensor")
    pieces = (
        lax.all_gather(k_rows, "seq", axis=1, tiled=True),
        lax.all_gather(value_rows, "seq", axis=1, tiled=True),
    )
    running_max = jnp.full((kv_heads, group_width, rows_here), -1e30, jnp.float32)
    block_rows = pieces[0].shape[1]
    key_block = pieces[0][0].reshape(block_rows, kv_heads, HEAD_SIZE)
    value_block = pieces[1][0].reshape(block_rows, kv_heads, HEAD_SIZE)
    scores = (
        jnp.einsum("igrd,jgd->grij", queries, key_block, preferred_element_type=jnp.float32)
        * softmax_scale
    )
    key_pos = jnp.arange(block_rows, dtype=jnp.int32)
    allowed = key_pos[None, :] <= query_pos[:, None]
    scores = jnp.where(allowed, scores, jnp.float32(-1e30))
    new_max = jnp.maximum(running_max, jnp.max(scores, axis=-1))
    weights = jnp.where(allowed, jnp.exp(scores - new_max[..., None]), jnp.float32(0.0))
    running_sum = jnp.sum(weights, axis=-1)
    weighted = jnp.einsum(
        "grij,jgd->grid",
        weights.astype(jnp.bfloat16),
        value_block,
        preferred_element_type=jnp.float32,
    )
    running_max, running_sum, weighted = (new_max, running_sum, weighted)
    attn_rows = (
        (weighted / running_sum[..., None])
        .transpose(2, 0, 1, 3)
        .reshape(rows_here, q_heads * HEAD_SIZE)
        .astype(jnp.bfloat16)
    )
    head_terms = jnp.dot(
        attn_rows,
        lax.all_gather(out_weight, "expert", axis=1, tiled=True),
        preferred_element_type=jnp.float32,
    )
    width = x_rows.shape[2]
    half_width = width // tensor_count
    share_sum = lax.psum_scatter(
        head_terms.astype(jnp.bfloat16), "tensor", scatter_dimension=1, tiled=True
    ).astype(jnp.float32)
    mixed_half = (
        lax.dynamic_slice_in_dim(x_rows[0], tensor_pos * half_width, half_width, 1).astype(
            jnp.float32
        )
        + share_sum
    )
    power = lax.psum(jnp.sum(mixed_half * mixed_half, axis=1), "tensor")
    inverse = lax.rsqrt(power / width + 1e-06)
    normed = (mixed_half * inverse[:, None] * norm_gain[None, :]).astype(jnp.bfloat16)
    seq_count = lax.axis_size("seq")
    group_count = lax.axis_size("expert")
    experts = seq_count * group_count
    capacity = max(2, 3 * rows_here * TOPK // (2 * experts))
    routed = expert_ids[0].reshape(-1)
    assigned = routed.shape[0]
    member = (routed[:, None] == jnp.arange(experts, dtype=jnp.int32)[None, :]).astype(jnp.int32)
    earlier = jnp.cumsum(member, axis=0) - member
    slot_index = jnp.sum(earlier * member, axis=1)
    target = routed * capacity + slot_index
    owner_index = (
        jnp.full((experts * capacity,), assigned, jnp.int32)
        .at[target]
        .set(jnp.arange(assigned, dtype=jnp.int32))
    )
    filled = owner_index < assigned
    source = jnp.minimum(owner_index // TOPK, rows_here - 1)
    outgoing = jnp.where(filled[:, None], normed[source], jnp.zeros((), jnp.bfloat16)).reshape(
        experts, capacity, half_width
    )
    arrived = lax.all_to_all(outgoing, ("seq", "expert"), split_axis=0, concat_axis=0, tiled=True)
    slot_count = arrived.shape[1]
    whole_rows = lax.all_gather(arrived, "tensor", axis=2, tiled=True)
    flat_rows = whole_rows.reshape(-1, whole_rows.shape[2])
    gate_act = jnp.dot(flat_rows, w_gate[0], preferred_element_type=jnp.float32)
    up_act = jnp.dot(flat_rows, w_up[0], preferred_element_type=jnp.float32)
    hidden = (jax.nn.silu(gate_act) * up_act).astype(jnp.bfloat16)
    partial_value = jnp.dot(hidden, w_down[0], preferred_element_type=jnp.float32).reshape(
        arrived.shape[0], slot_count, whole_rows.shape[2]
    )
    returned = lax.all_to_all(
        lax.psum_scatter(
            partial_value.astype(jnp.bfloat16), "tensor", scatter_dimension=2, tiled=True
        ),
        ("seq", "expert"),
        split_axis=0,
        concat_axis=0,
        tiled=True,
    )
    came_back = returned.reshape(experts * capacity, half_width)
    picked = came_back[target].astype(jnp.float32)
    weights_flat = gate_weights[0].reshape(-1)
    blended = jnp.sum((picked * weights_flat[:, None]).reshape(rows_here, TOPK, half_width), axis=1)
    return (mixed_half + blended).astype(jnp.bfloat16)[None]


def bits_of(size):
    return [1 << n for n in range(size.bit_length() - 1)]


def swap(value, axis, bit):
    count = lax.axis_size(axis)
    return lax.ppermute(value, axis, [(i, i ^ bit) for i in range(count)])


def slot_order(bits):
    order = [0]
    for bit in bits:
        order = order + [place ^ bit for place in order]
    return order


def gather_slots(value, axis, bits):
    held = value[None]
    for bit in bits:
        held = jnp.concatenate([held, swap(held, axis, bit)], axis=0)
    return held


def gather_parts(value, axis, bits):
    held = [value]
    for bit in bits:
        arrived = []
        for part in held:
            arrived.append(swap(part, axis, bit))
        held = held + arrived
    return held


def total(terms):
    if len(terms) == 1:
        return terms[0]
    return sum(term.astype(jnp.float32) for term in terms).astype(terms[0].dtype)


def return_parts(parts, axis, bits):
    held = [[part] for part in parts]
    for bit in reversed(bits):
        half = len(held) // 2
        arrived = [None] * half
        for i in reversed(range(half)):
            arrived[i] = swap(total(held[half + i]), axis, bit)
        held = [terms + [extra] for terms, extra in zip(held, arrived)]
    return held[0]


def return_rows(terms, axis, bits):
    for bit in reversed(bits):
        half = terms[0].shape[0] // 2
        arrived = swap(total([term[half:] for term in terms]), axis, bit)
        terms = [term[:half] for term in terms] + [arrived]
    return [term[0] for term in terms]


def expert_kernel(order, near, start_row, *refs):
    groups = len(order)
    refs = list(refs)
    place_ref, table_ref, w_in_ref, w_out_ref = refs[:4]
    in_refs, refs = refs[4 : 4 + groups], refs[4 + groups :]
    halves, blocks, sessions, rows, piece = in_refs[0].shape
    gain_refs, refs = refs[:halves], refs[halves:]
    proj_ref, received_ref = (None, None) if near else (refs.pop(0), refs.pop(0))
    normed_ref, gain_ref = refs.pop(-2), refs.pop()
    half_width = refs[0].shape[-1]
    width = half_width * halves
    hidden_width = w_out_ref.shape[0]
    me, half_me, seq_me = place_ref[0], place_ref[1], place_ref[2]
    per_half = half_width // piece
    count = groups * rows * blocks
    for k, ref in enumerate(gain_refs):
        gain_ref[k * per_half : (k + 1) * per_half] = ref[...]

    power = jnp.zeros((count, 1), jnp.float32)
    pieces = []
    for i, in_ref in enumerate(in_refs):
        for k in range(halves):
            tokens = jnp.concatenate(
                [
                    in_ref[k, b, lax.bitwise_xor(me, order[r])]
                    for b in range(blocks)
                    for r in range(groups)
                ],
                axis=0,
            )
            mixed = tokens.astype(jnp.float32)
            power = power + jnp.sum(mixed * mixed, axis=1, keepdims=True)
            pieces.append((i, k, tokens))
    inverse = lax.rsqrt(power * (1.0 / width) + 1e-06)
    for i, k, tokens in pieces:
        spot = lax.bitwise_xor(me, order[i]) * halves + lax.bitwise_xor(half_me, k)
        away = lax.bitwise_xor(lax.div(spot, per_half), half_me)
        gain = gain_ref[pl.ds(away * per_half + lax.rem(spot, per_half), 1), :]
        normed_ref[:, pl.ds(pl.multiple_of(spot * piece, piece), piece)] = (
            tokens.astype(jnp.float32) * inverse * gain
        ).astype(jnp.bfloat16)
    both = jnp.dot(normed_ref[...], w_in_ref[...], preferred_element_type=jnp.float32)
    gate_act, up_act = both[:, :hidden_width], both[:, hidden_width:]
    hidden = (gate_act / (1.0 + jnp.exp(-gate_act)) * up_act).astype(jnp.bfloat16)

    diagonal = lax.broadcasted_iota(jnp.int32, (rows, rows), 0) == lax.broadcasted_iota(
        jnp.int32, (rows, rows), 1
    )
    scales = []
    for b in range(blocks):
        for r in range(groups):
            source = lax.bitwise_xor(seq_me, 2 * b + near) * sessions
            source = source + lax.bitwise_xor(me, order[r])
            line = table_ref[pl.ds(source, 1), :][:, start_row : start_row + rows]
            scales.append(
                jnp.sum(jnp.where(diagonal, line, 0.0), axis=1, keepdims=True)
            )
    scale = jnp.concatenate(scales, axis=0)
    for half in range(halves):
        k = lax.bitwise_xor(half_me, half)
        result = scale * jnp.dot(
            hidden,
            w_out_ref[:, half * half_width : (half + 1) * half_width],
            preferred_element_type=jnp.float32,
        )
        at = 0
        for b in range(blocks):
            for r in range(groups):
                part = result[at : at + rows]
                at += rows
                if proj_ref is not None and b == 0:
                    proj = proj_ref[order[r], start_row : start_row + rows]
                    columns = []
                    for m in range(per_half):
                        mine = me * halves + half_me == half * per_half + m
                        columns.append(
                            part[:, m * piece : (m + 1) * piece]
                            + proj * mine.astype(jnp.float32)
                        )
                    part = jnp.concatenate(columns, axis=1)
                if received_ref is not None:
                    part = part + received_ref[r, k, b].astype(jnp.float32)
                part = part.astype(jnp.bfloat16)
                if near:
                    refs[0][r, k, b] = part
                else:
                    refs[r][k, b] = part


def attention_kernel(head, order, place_ref, q_ref, *refs):
    slots = len(order)
    k_refs, v_refs, out_ref = refs[:slots], refs[slots : 2 * slots], refs[-1]
    rows = q_ref.shape[0]
    columns = slice(head * HEAD_SIZE, (head + 1) * HEAD_SIZE)
    keys = jnp.concatenate([ref[:, columns] for ref in k_refs], axis=0)
    values = jnp.concatenate([ref[:, columns] for ref in v_refs], axis=0)
    down = lax.broadcasted_iota(jnp.int32, (rows, rows), 0)
    across = lax.broadcasted_iota(jnp.int32, (rows, rows), 1)
    seq_me = place_ref[2]
    allowed = jnp.concatenate(
        [
            (lax.bitwise_xor(seq_me, place) - seq_me) * rows + across <= down
            for place in order
        ],
        axis=1,
    )
    heads = out_ref.shape[1] // HEAD_SIZE
    batch = max(1, heads // 2)
    allowed = jnp.concatenate([allowed] * batch, axis=0)
    for first in range(0, heads, batch):
        start = head * heads + first
        queries = jnp.concatenate(
            [
                q_ref[:, (start + n) * HEAD_SIZE : (start + n + 1) * HEAD_SIZE]
                for n in range(batch)
            ],
            axis=0,
        )
        scores = lax.dot_general(
            queries, keys, (((1,), (1,)), ((), ())), preferred_element_type=jnp.float32
        ) * (1.0 / math.sqrt(HEAD_SIZE))
        scores = jnp.where(allowed, scores, jnp.float32(-1e30))
        weights = jnp.exp(scores - jnp.max(scores, axis=1, keepdims=True))
        mixed = jnp.dot(
            weights.astype(jnp.bfloat16), values, preferred_element_type=jnp.float32
        )
        mixed = (mixed / jnp.sum(weights, axis=1, keepdims=True)).astype(jnp.bfloat16)
        for n in range(batch):
            out_ref[:, (first + n) * HEAD_SIZE : (first + n + 1) * HEAD_SIZE] = mixed[
                n * rows : (n + 1) * rows
            ]


def side_kernel(place_ref, x_ref, ids_ref, weights_ref, table_ref, half_ref, *piece_refs):
    me, half_me = place_ref[0], place_ref[1]
    width, half_width, piece = (ref.shape[1] for ref in (x_ref, half_ref, piece_refs[0]))
    halves = width // half_width
    start = pl.multiple_of(half_me * half_width, half_width)
    half_ref[...] = x_ref[:, pl.ds(start, half_width)]
    for r, piece_ref in enumerate(piece_refs):
        spot = lax.bitwise_xor(me, r) * halves + half_me
        piece_ref[...] = x_ref[:, pl.ds(pl.multiple_of(spot * piece, piece), piece)]
    number = lax.broadcasted_iota(jnp.int32, (x_ref.shape[0], LANES), 1)
    table = jnp.zeros(number.shape, jnp.float32)
    for k in range(ids_ref.shape[1]):
        table += jnp.where(ids_ref[:, k : k + 1] == number, weights_ref[:, k : k + 1], 0.0)
    table_ref[...] = table.T[: table_ref.shape[0]]


def project_kernel(away, place_ref, w_ref, *refs):
    out_ref, joined_ref = refs[-2:]
    sessions, rows, piece = out_ref.shape
    depth = refs[0].shape[1]
    for n, ref in enumerate(refs[:-2]):
        half, r = divmod(n, sessions)
        joined_ref[r * rows : (r + 1) * rows, half * depth : (half + 1) * depth] = ref[...]
    start = pl.multiple_of(lax.bitwise_xor(place_ref[1], away) * piece, piece)
    result = jnp.dot(
        joined_ref[...], w_ref[:, pl.ds(start, piece)], preferred_element_type=jnp.float32
    )
    out_ref[...] = result.reshape(sessions, rows, piece).astype(out_ref.dtype)


def mix_kernel(sessions, place_ref, *refs):
    x_refs, refs = refs[:sessions], refs[sessions:]
    terms, (proj_ref, *chunk_refs) = refs[: -1 - CHUNKS], refs[-1 - CHUNKS :]
    rows = chunk_refs[0].shape[1]
    me = place_ref[0]
    for r in range(sessions):
        proj = sum(ref[r].astype(jnp.float32) for ref in terms)
        proj_ref[r] = proj
        mixed = (x_refs[r][...].astype(jnp.float32) + proj).astype(jnp.bfloat16)
        for c, chunk_ref in enumerate(chunk_refs):
            chunk_ref[lax.bitwise_xor(me, r)] = mixed[c * rows : (c + 1) * rows]


def local_kernel(kernel, outs, operands, scratch=(), limit=8 << 20):
    return pl.pallas_call(
        kernel,
        out_shape=outs,
        in_specs=[pl.BlockSpec(memory_space=pltpu.SMEM)]
        + [pl.BlockSpec(memory_space=pltpu.VMEM)] * (len(operands) - 1),
        out_specs=[pl.BlockSpec(memory_space=pltpu.VMEM)] * len(outs),
        scratch_shapes=scratch,
        compiler_params=pltpu.CompilerParams(vmem_limit_bytes=limit),
    )(*operands)


def dense_plan(
    q_rows,
    k_rows,
    value_rows,
    x_rows,
    out_weight,
    norm_gain,
    w_gate,
    w_up,
    w_down,
    expert_ids,
    gate_weights,
):
    rows_here = q_rows.shape[1]
    width = x_rows.shape[2]
    seq_count, group_count = lax.axis_size("seq"), lax.axis_size("expert")
    tensor_count = lax.axis_size("tensor")
    experts = seq_count * group_count
    seq_pos, group_pos = lax.axis_index("seq"), lax.axis_index("expert")
    tensor_pos = lax.axis_index("tensor")
    seq_bits, group_bits = bits_of(seq_count), bits_of(group_count)
    tensor_bits = bits_of(tensor_count)
    half_width = width // tensor_count
    piece = width // (group_count * tensor_count)
    near, far = seq_bits[:1], seq_bits[1:]

    place = jnp.stack([group_pos, tensor_pos, seq_pos]).astype(jnp.int32)

    kv_bits = far + near
    keys = gather_parts(k_rows[0], "seq", kv_bits)
    values = gather_parts(value_rows[0], "seq", kv_bits)

    piece_type = jax.ShapeDtypeStruct((rows_here, piece), x_rows.dtype)
    table, x_half, *x_slots = local_kernel(
        side_kernel,
        [
            jax.ShapeDtypeStruct((experts, rows_here), jnp.float32),
            jax.ShapeDtypeStruct((rows_here, half_width), x_rows.dtype),
        ]
        + [piece_type] * group_count,
        [place, x_rows[0], expert_ids[0], gate_weights[0]],
    )
    for r in range(1, group_count):
        x_slots[r] = swap(x_slots[r], "expert", r)
    table = lax.all_to_all(table, ("seq", "expert"), split_axis=0, concat_axis=0, tiled=True)
    gain = norm_gain.reshape(half_width // piece, piece)
    place, table, gain = lax.optimization_barrier((place, table, gain))

    kv_heads = k_rows.shape[2] // HEAD_SIZE
    depth = q_rows.shape[2] // kv_heads
    attended = []
    for head in range(kv_heads):
        attended += local_kernel(
            functools.partial(attention_kernel, head, tuple(slot_order(kv_bits))),
            [jax.ShapeDtypeStruct((rows_here, depth), jnp.bfloat16)],
            [place, q_rows[0], *keys, *values],
        )

    w_gate, w_up, gain, _ = lax.optimization_barrier((w_gate, w_up, gain, attended[0]))
    gains = gather_parts(gain, "tensor", tensor_bits)
    w_in = jnp.concatenate([w_gate[0], w_up[0]], axis=1)

    paths = (group_bits, group_bits[::-1])
    gathered = []
    for n, rows_of in enumerate(attended):
        path = paths[n % len(paths)]
        held = gather_parts(rows_of, "expert", path)
        order = slot_order(path)
        gathered += [held[order.index(r)] for r in range(group_count)]

    def projected(k, kind):
        shape = (group_count, rows_here, piece)
        return local_kernel(
            functools.partial(project_kernel, k),
            [jax.ShapeDtypeStruct(shape, kind)],
            [place, out_weight, *gathered],
            [pltpu.VMEM((group_count * rows_here, out_weight.shape[0]), jnp.bfloat16)],
        )[0]

    terms = []
    for k in range(1, tensor_count):
        away = projected(k, jnp.bfloat16)
        terms.append(swap(away, "tensor", k))
    terms.append(projected(0, jnp.float32))
    rows = rows_here // CHUNKS
    part = jax.ShapeDtypeStruct((group_count, rows, piece), jnp.bfloat16)
    proj, *by_session = local_kernel(
        functools.partial(mix_kernel, group_count),
        [jax.ShapeDtypeStruct((group_count, rows_here, piece), jnp.float32)] + [part] * CHUNKS,
        [place, *x_slots, *terms],
    )
    w_in, *rest = lax.optimization_barrier((w_in, *gains, *by_session))
    gains, by_session = rest[:tensor_count], rest[tensor_count:]

    blocks = seq_count // 2
    chunks = []
    for c in range(CHUNKS):
        path = paths[c % len(paths)]
        held = by_session[c]
        held = gather_slots(held, "seq", far)
        held = gather_slots(held, "tensor", tensor_bits)
        own = gather_parts(held, "expert", path)
        other = []
        for part in own:
            other.append(swap(part, "seq", near[0]))
        chunks.append((c, path, own, other))

    def experts_on(c, path, parts, received):
        order = tuple(slot_order(path))
        operands = [place, table, w_in, w_down[0], *parts, *gains]
        shape = (tensor_count, blocks, rows, half_width)
        if received is None:
            shapes = [jax.ShapeDtypeStruct((group_count, *shape), jnp.bfloat16)]
        else:
            operands += [proj, received]
            shapes = [jax.ShapeDtypeStruct(shape, jnp.bfloat16)] * group_count
        near_order = near[0] if received is None else 0
        return local_kernel(
            functools.partial(expert_kernel, order, near_order, c * rows),
            shapes,
            operands,
            [
                pltpu.VMEM((group_count * blocks * rows, width), jnp.bfloat16),
                pltpu.VMEM((width // piece, piece), jnp.float32),
            ],
            KERNEL_BYTES,
        )

    finished = []
    for c, path, own, other in chunks:
        (away,) = experts_on(c, path, other, None)
        away = swap(away, "seq", near[0])
        parts = experts_on(c, path, own, away)
        terms = return_parts(parts, "expert", path)
        terms = return_rows(terms, "tensor", tensor_bits)
        terms = return_rows(terms, "seq", far)
        finished.append(sum(term.astype(jnp.float32) for term in terms))
    summed = jnp.concatenate(finished, axis=0)
    return (x_half.astype(jnp.float32) + summed).astype(jnp.bfloat16)[None]


def per_device(*arrays):
    rows_here = arrays[0].shape[1]
    counts = [lax.axis_size(axis) for axis in ("seq", "expert", "tensor")]
    experts = counts[0] * counts[1]
    capacity = max(2, 3 * rows_here * TOPK // (2 * experts))
    dense = experts * rows_here <= 2 * experts * capacity
    regular = all(count > 1 and count & (count - 1) == 0 for count in counts)
    fits = experts <= LANES and rows_here % (16 * CHUNKS) == 0
    if dense and regular and fits:
        return dense_plan(*arrays)
    return dispatch_plan(*arrays)


def solution(mesh):
    return jax.shard_map(
        per_device,
        mesh=mesh,
        in_specs=(
            P("expert", "seq", "tensor"),
            P("expert", "seq", "tensor"),
            P("expert", "seq", "tensor"),
            P("expert", "seq", None),
            P("tensor", "expert"),
            P("tensor"),
            P(("seq", "expert"), None, "tensor"),
            P(("seq", "expert"), None, "tensor"),
            P(("seq", "expert"), "tensor", None),
            P("expert", "seq", None),
            P("expert", "seq", None),
        ),
        out_specs=P("expert", "seq", "tensor"),
        check_vma=False,
    )
```

```python
import functools
import math

import jax
import jax.numpy as jnp
from jax import lax
from jax.experimental import pallas as pl
from jax.experimental.pallas import tpu as pltpu
from jax.sharding import PartitionSpec as P


HEAD_SIZE = 128
TOPK = 8
LANES = 128
CHUNKS = 4
KERNEL_BYTES = 6 << 20


def dispatch_plan(
    q_rows,
    k_rows,
    value_rows,
    x_rows,
    out_weight,
    norm_gain,
    w_gate,
    w_up,
    w_down,
    expert_ids,
    gate_weights,
):
    rows_here = q_rows.shape[1]
    kv_heads = k_rows.shape[2] // HEAD_SIZE
    q_heads = q_rows.shape[2] // HEAD_SIZE
    group_width = q_heads // kv_heads
    queries = q_rows[0].reshape(rows_here, kv_heads, group_width, HEAD_SIZE)
    offset = lax.axis_index("seq") * rows_here
    query_pos = offset + jnp.arange(rows_here, dtype=jnp.int32)
    softmax_scale = 1.0 / math.sqrt(HEAD_SIZE)
    tensor_pos = lax.axis_index("tensor")
    tensor_count = lax.axis_size("tensor")
    pieces = (
        lax.all_gather(k_rows, "seq", axis=1, tiled=True),
        lax.all_gather(value_rows, "seq", axis=1, tiled=True),
    )
    running_max = jnp.full((kv_heads, group_width, rows_here), -1e30, jnp.float32)
    block_rows = pieces[0].shape[1]
    key_block = pieces[0][0].reshape(block_rows, kv_heads, HEAD_SIZE)
    value_block = pieces[1][0].reshape(block_rows, kv_heads, HEAD_SIZE)
    scores = (
        jnp.einsum("igrd,jgd->grij", queries, key_block, preferred_element_type=jnp.float32)
        * softmax_scale
    )
    key_pos = jnp.arange(block_rows, dtype=jnp.int32)
    allowed = key_pos[None, :] <= query_pos[:, None]
    scores = jnp.where(allowed, scores, jnp.float32(-1e30))
    new_max = jnp.maximum(running_max, jnp.max(scores, axis=-1))
    weights = jnp.where(allowed, jnp.exp(scores - new_max[..., None]), jnp.float32(0.0))
    running_sum = jnp.sum(weights, axis=-1)
    weighted = jnp.einsum(
        "grij,jgd->grid",
        weights.astype(jnp.bfloat16),
        value_block,
        preferred_element_type=jnp.float32,
    )
    running_max, running_sum, weighted = (new_max, running_sum, weighted)
    attn_rows = (
        (weighted / running_sum[..., None])
        .transpose(2, 0, 1, 3)
        .reshape(rows_here, q_heads * HEAD_SIZE)
        .astype(jnp.bfloat16)
    )
    head_terms = jnp.dot(
        attn_rows,
        lax.all_gather(out_weight, "expert", axis=1, tiled=True),
        preferred_element_type=jnp.float32,
    )
    width = x_rows.shape[2]
    half_width = width // tensor_count
    share_sum = lax.psum_scatter(
        head_terms.astype(jnp.bfloat16), "tensor", scatter_dimension=1, tiled=True
    ).astype(jnp.float32)
    mixed_half = (
        lax.dynamic_slice_in_dim(x_rows[0], tensor_pos * half_width, half_width, 1).astype(
            jnp.float32
        )
        + share_sum
    )
    power = lax.psum(jnp.sum(mixed_half * mixed_half, axis=1), "tensor")
    inverse = lax.rsqrt(power / width + 1e-06)
    normed = (mixed_half * inverse[:, None] * norm_gain[None, :]).astype(jnp.bfloat16)
    seq_count = lax.axis_size("seq")
    group_count = lax.axis_size("expert")
    experts = seq_count * group_count
    capacity = max(2, 3 * rows_here * TOPK // (2 * experts))
    routed = expert_ids[0].reshape(-1)
    assigned = routed.shape[0]
    member = (routed[:, None] == jnp.arange(experts, dtype=jnp.int32)[None, :]).astype(jnp.int32)
    earlier = jnp.cumsum(member, axis=0) - member
    slot_index = jnp.sum(earlier * member, axis=1)
    target = routed * capacity + slot_index
    owner_index = (
        jnp.full((experts * capacity,), assigned, jnp.int32)
        .at[target]
        .set(jnp.arange(assigned, dtype=jnp.int32))
    )
    filled = owner_index < assigned
    source = jnp.minimum(owner_index // TOPK, rows_here - 1)
    outgoing = jnp.where(filled[:, None], normed[source], jnp.zeros((), jnp.bfloat16)).reshape(
        experts, capacity, half_width
    )
    arrived = lax.all_to_all(outgoing, ("seq", "expert"), split_axis=0, concat_axis=0, tiled=True)
    slot_count = arrived.shape[1]
    whole_rows = lax.all_gather(arrived, "tensor", axis=2, tiled=True)
    flat_rows = whole_rows.reshape(-1, whole_rows.shape[2])
    gate_act = jnp.dot(flat_rows, w_gate[0], preferred_element_type=jnp.float32)
    up_act = jnp.dot(flat_rows, w_up[0], preferred_element_type=jnp.float32)
    hidden = (jax.nn.silu(gate_act) * up_act).astype(jnp.bfloat16)
    partial_value = jnp.dot(hidden, w_down[0], preferred_element_type=jnp.float32).reshape(
        arrived.shape[0], slot_count, whole_rows.shape[2]
    )
    returned = lax.all_to_all(
        lax.psum_scatter(
            partial_value.astype(jnp.bfloat16), "tensor", scatter_dimension=2, tiled=True
        ),
        ("seq", "expert"),
        split_axis=0,
        concat_axis=0,
        tiled=True,
    )
    came_back = returned.reshape(experts * capacity, half_width)
    picked = came_back[target].astype(jnp.float32)
    weights_flat = gate_weights[0].reshape(-1)
    blended = jnp.sum((picked * weights_flat[:, None]).reshape(rows_here, TOPK, half_width), axis=1)
    return (mixed_half + blended).astype(jnp.bfloat16)[None]


def bits_of(size):
    return [1 << n for n in range(size.bit_length() - 1)]


def swap(value, axis, bit):
    count = lax.axis_size(axis)
    return lax.ppermute(value, axis, [(i, i ^ bit) for i in range(count)])


def slot_order(bits):
    order = [0]
    for bit in bits:
        order = order + [place ^ bit for place in order]
    return order


def gather_slots(value, axis, bits):
    held = value[None]
    for bit in bits:
        held = jnp.concatenate([held, swap(held, axis, bit)], axis=0)
    return held


def gather_parts(value, axis, bits):
    held = [value]
    for bit in bits:
        arrived = []
        for part in held:
            arrived.append(swap(part, axis, bit))
        held = held + arrived
    return held


def exchange_rows(table, steps):
    lanes = table.shape[1]
    sizes = {"seq": lax.axis_size("seq"), "expert": lax.axis_size("expert")}
    table = table.reshape(sizes["seq"], sizes["expert"], lanes)
    for axis, bit in steps:
        dim = 0 if axis == "seq" else 1
        size = sizes[axis]
        parts = jnp.split(table, size, axis=dim)
        low = [n for n in range(size) if not n & bit]
        away = jnp.concatenate([parts[n ^ bit] for n in low], axis=dim)
        away = swap(away, axis, bit)
        arrived = jnp.split(away, len(low), axis=dim)
        for n, part in zip(low, arrived):
            parts[n ^ bit] = part
        table = jnp.concatenate(parts, axis=dim)
    return table.reshape(-1, lanes)


def total(terms):
    if len(terms) == 1:
        return terms[0]
    return sum(term.astype(jnp.float32) for term in terms).astype(terms[0].dtype)


def return_parts(parts, axis, bits):
    held = [[part] for part in parts]
    for bit in reversed(bits):
        half = len(held) // 2
        arrived = [None] * half
        for i in reversed(range(half)):
            arrived[i] = swap(total(held[half + i]), axis, bit)
        held = [terms + [extra] for terms, extra in zip(held, arrived)]
    return held[0]


def return_rows(terms, axis, bits):
    for bit in reversed(bits):
        half = terms[0].shape[0] // 2
        arrived = swap(total([term[half:] for term in terms]), axis, bit)
        terms = [term[:half] for term in terms] + [arrived]
    return [term[0] for term in terms]


def expert_kernel(order, near, start_row, *refs):
    groups = len(order)
    refs = list(refs)
    table_ref, w_in_ref, w_out_ref = refs[:3]
    in_refs, refs = refs[3 : 3 + groups], refs[3 + groups :]
    halves, blocks, sessions, rows, piece = in_refs[0].shape
    gain_refs, refs = refs[:halves], refs[halves:]
    proj_ref, received_ref = (None, None) if near else (refs.pop(0), refs.pop(0))
    normed_ref, gain_ref = refs.pop(-2), refs.pop()
    half_width = refs[0].shape[-1]
    width = half_width * halves
    hidden_width = w_out_ref.shape[0]
    me, half_me = lax.axis_index("expert"), lax.axis_index("tensor")
    per_half = half_width // piece
    count = groups * rows * blocks
    for k, ref in enumerate(gain_refs):
        for n in range(per_half):
            for lane in range(0, piece, LANES):
                line = (n * piece + lane) // LANES
                gain_ref[k * per_half + n : k * per_half + n + 1, lane : lane + LANES] = ref[
                    line : line + 1
                ]

    power = jnp.zeros((count, 1), jnp.float32)
    pieces = []
    for i, in_ref in enumerate(in_refs):
        for k in range(halves):
            tokens = jnp.concatenate(
                [
                    in_ref[k, b, lax.bitwise_xor(me, order[r])]
                    for b in range(blocks)
                    for r in range(groups)
                ],
                axis=0,
            )
            mixed = tokens.astype(jnp.float32)
            power = power + jnp.sum(mixed * mixed, axis=1, keepdims=True)
            pieces.append((i, k, tokens))
    inverse = lax.rsqrt(power * (1.0 / width) + 1e-06)
    for i, k, tokens in pieces:
        spot = lax.bitwise_xor(me, order[i]) * halves + lax.bitwise_xor(half_me, k)
        away = lax.bitwise_xor(lax.div(spot, per_half), half_me)
        gain = gain_ref[pl.ds(away * per_half + lax.rem(spot, per_half), 1), :]
        normed_ref[:, pl.ds(pl.multiple_of(spot * piece, piece), piece)] = (
            tokens.astype(jnp.float32) * inverse * gain
        ).astype(jnp.bfloat16)
    both = jnp.dot(normed_ref[...], w_in_ref[...], preferred_element_type=jnp.float32)
    gate_act, up_act = both[:, :hidden_width], both[:, hidden_width:]
    hidden = (gate_act / (1.0 + jnp.exp(-gate_act)) * up_act).astype(jnp.bfloat16)

    diagonal = lax.broadcasted_iota(jnp.int32, (rows, rows), 0) == lax.broadcasted_iota(
        jnp.int32, (rows, rows), 1
    )
    scales = []
    for b in range(blocks):
        for r in range(groups):
            source = (2 * b + near) * sessions + order[r]
            line = table_ref[source : source + 1, start_row : start_row + rows]
            scales.append(
                jnp.sum(jnp.where(diagonal, line, 0.0), axis=1, keepdims=True)
            )
    scale = jnp.concatenate(scales, axis=0)
    for half in range(halves):
        k = lax.bitwise_xor(half_me, half)
        result = scale * jnp.dot(
            hidden,
            w_out_ref[:, half * half_width : (half + 1) * half_width],
            preferred_element_type=jnp.float32,
        )
        at = 0
        for b in range(blocks):
            for r in range(groups):
                part = result[at : at + rows]
                at += rows
                if proj_ref is not None and b == 0:
                    proj = proj_ref[order[r], start_row : start_row + rows]
                    columns = []
                    for m in range(per_half):
                        mine = me * halves + half_me == half * per_half + m
                        columns.append(
                            part[:, m * piece : (m + 1) * piece]
                            + proj * mine.astype(jnp.float32)
                        )
                    part = jnp.concatenate(columns, axis=1)
                if received_ref is not None:
                    part = part + received_ref[r, k, b].astype(jnp.float32)
                part = part.astype(jnp.bfloat16)
                if near:
                    refs[0][r, k, b] = part
                else:
                    refs[r][k, b] = part


def attention_kernel(head, order, q_ref, *refs):
    slots = len(order)
    k_refs, v_refs, out_ref = refs[:slots], refs[slots : 2 * slots], refs[-1]
    rows = q_ref.shape[0]
    columns = slice(head * HEAD_SIZE, (head + 1) * HEAD_SIZE)
    keys = jnp.concatenate([ref[:, columns] for ref in k_refs], axis=0)
    values = jnp.concatenate([ref[:, columns] for ref in v_refs], axis=0)
    down = lax.broadcasted_iota(jnp.int32, (rows, rows), 0)
    across = lax.broadcasted_iota(jnp.int32, (rows, rows), 1)
    seq_me = lax.axis_index("seq")
    allowed = jnp.concatenate(
        [
            (lax.bitwise_xor(seq_me, place) - seq_me) * rows + across <= down
            for place in order
        ],
        axis=1,
    )
    heads = out_ref.shape[1] // HEAD_SIZE
    batch = max(1, heads // 2)
    allowed = jnp.concatenate([allowed] * batch, axis=0)
    for first in range(0, heads, batch):
        queries = jnp.concatenate(
            [
                q_ref[:, (first + n) * HEAD_SIZE : (first + n + 1) * HEAD_SIZE]
                for n in range(batch)
            ],
            axis=0,
        )
        scores = lax.dot_general(
            queries, keys, (((1,), (1,)), ((), ())), preferred_element_type=jnp.float32
        ) * (1.0 / math.sqrt(HEAD_SIZE))
        scores = jnp.where(allowed, scores, jnp.float32(-1e30))
        weights = jnp.exp(scores - jnp.max(scores, axis=1, keepdims=True))
        mixed = jnp.dot(
            weights.astype(jnp.bfloat16), values, preferred_element_type=jnp.float32
        )
        mixed = (mixed / jnp.sum(weights, axis=1, keepdims=True)).astype(jnp.bfloat16)
        for n in range(batch):
            out_ref[:, (first + n) * HEAD_SIZE : (first + n + 1) * HEAD_SIZE] = mixed[
                n * rows : (n + 1) * rows
            ]


def side_kernel(groups, x_ref, q_ref, k_ref, v_ref, ids_ref, weights_ref, *refs):
    ids, weights, sems = refs[-3:]
    table_ref, half_ref, k_out, v_out = refs[:4]
    piece_refs, q_outs = refs[4 : 4 + groups], refs[4 + groups : -3]
    me, half_me, seq_me = (lax.axis_index(name) for name in ("expert", "tensor", "seq"))
    width, half_width, piece = (ref.shape[1] for ref in (x_ref, half_ref, piece_refs[0]))
    moves = [(ids_ref, ids), (weights_ref, weights)]
    for r, piece_ref in enumerate(piece_refs):
        spot = lax.bitwise_xor(me, r) * (width // half_width) + half_me
        start = pl.multiple_of(spot * piece, piece)
        moves.append((x_ref.at[:, pl.ds(start, piece)], piece_ref))
    moves += [(k_ref, k_out), (v_ref, v_out)]
    depth = q_outs[0].shape[1]
    for n, out in enumerate(q_outs):
        moves.append((q_ref.at[:, n * depth : (n + 1) * depth], out))
    start = pl.multiple_of(half_me * half_width, half_width)
    moves.append((x_ref.at[:, pl.ds(start, half_width)], half_ref))
    copies = [
        pltpu.make_async_copy(source, target, sems.at[n])
        for n, (source, target) in enumerate(moves)
    ]
    for copy in copies:
        copy.start()
    copies[0].wait()
    copies[1].wait()
    for n in range(table_ref.shape[0]):
        expert = lax.bitwise_xor(seq_me, n // groups) * groups
        expert = expert + lax.bitwise_xor(me, n % groups)
        table_ref[n : n + 1] = jnp.sum(
            jnp.where(ids[...] == expert, weights[...], 0.0), axis=0, keepdims=True
        )
    for copy in copies[2:]:
        copy.wait()


def project_kernel(away, w_ref, *refs):
    out_ref, joined_ref = refs[-2:]
    sessions, rows, piece = out_ref.shape
    depth = refs[0].shape[1]
    for n, ref in enumerate(refs[:-2]):
        half, r = divmod(n, sessions)
        joined_ref[r * rows : (r + 1) * rows, half * depth : (half + 1) * depth] = ref[...]
    start = pl.multiple_of(lax.bitwise_xor(lax.axis_index("tensor"), away) * piece, piece)
    result = jnp.dot(
        joined_ref[...], w_ref[:, pl.ds(start, piece)], preferred_element_type=jnp.float32
    )
    out_ref[...] = result.reshape(sessions, rows, piece).astype(out_ref.dtype)


def mix_kernel(sessions, *refs):
    x_refs, refs = refs[:sessions], refs[sessions:]
    terms, (proj_ref, *chunk_refs) = refs[: -1 - CHUNKS], refs[-1 - CHUNKS :]
    rows = chunk_refs[0].shape[1]
    me = lax.axis_index("expert")
    for r in range(sessions):
        proj = sum(ref[r].astype(jnp.float32) for ref in terms)
        proj_ref[r] = proj
        mixed = (x_refs[r][...].astype(jnp.float32) + proj).astype(jnp.bfloat16)
        for c, chunk_ref in enumerate(chunk_refs):
            chunk_ref[lax.bitwise_xor(me, r)] = mixed[c * rows : (c + 1) * rows]


def local_kernel(kernel, outs, operands, scratch=(), limit=8 << 20, space=pltpu.VMEM):
    return pl.pallas_call(
        kernel,
        out_shape=outs,
        in_specs=[pl.BlockSpec(memory_space=space)] * len(operands),
        out_specs=[pl.BlockSpec(memory_space=pltpu.VMEM)] * len(outs),
        scratch_shapes=scratch,
        compiler_params=pltpu.CompilerParams(vmem_limit_bytes=limit),
    )(*operands)


def dense_plan(
    q_rows,
    k_rows,
    value_rows,
    x_rows,
    out_weight,
    norm_gain,
    w_gate,
    w_up,
    w_down,
    expert_ids,
    gate_weights,
):
    rows_here = q_rows.shape[1]
    width = x_rows.shape[2]
    seq_count, group_count = lax.axis_size("seq"), lax.axis_size("expert")
    tensor_count = lax.axis_size("tensor")
    experts = seq_count * group_count
    seq_bits, group_bits = bits_of(seq_count), bits_of(group_count)
    tensor_bits = bits_of(tensor_count)
    half_width = width // tensor_count
    piece = width // (group_count * tensor_count)
    near, far = seq_bits[:1], seq_bits[1:]

    kv_bits = far + near
    keys = gather_parts(k_rows[0], "seq", kv_bits)
    values = gather_parts(value_rows[0], "seq", kv_bits)

    kv_heads = k_rows.shape[2] // HEAD_SIZE
    depth = q_rows.shape[2] // kv_heads
    kind = x_rows.dtype
    ids, weights = expert_ids[0].T, gate_weights[0].T
    shapes = [(experts, rows_here), (rows_here, half_width)]
    shapes += [k_rows.shape[1:]] * 2 + [(rows_here, piece)] * group_count
    shapes += [(rows_here, depth)] * kv_heads
    table, x_half, keys[0], values[0], *rest = local_kernel(
        functools.partial(side_kernel, group_count),
        [jax.ShapeDtypeStruct(shape, kind if n else jnp.float32) for n, shape in enumerate(shapes)],
        [x_rows[0], q_rows[0], k_rows[0], value_rows[0], ids, weights],
        [
            pltpu.VMEM(ids.shape, ids.dtype),
            pltpu.VMEM(weights.shape, weights.dtype),
            pltpu.SemaphoreType.DMA((len(shapes) + 1,)),
        ],
        space=pltpu.HBM,
    )
    x_slots, queries = rest[:group_count], rest[group_count:]
    for r in range(1, group_count):
        x_slots[r] = swap(x_slots[r], "expert", r)
    gain = norm_gain.reshape(half_width // LANES, LANES)

    attended = []
    for head in range(kv_heads):
        attended += local_kernel(
            functools.partial(attention_kernel, head, tuple(slot_order(kv_bits))),
            [jax.ShapeDtypeStruct((rows_here, depth), jnp.bfloat16)],
            [queries[head], *keys, *values],
        )

    w_gate, w_up, gain, table, _ = lax.optimization_barrier(
        (w_gate, w_up, gain, table, attended[0])
    )
    table = exchange_rows(
        table, [("seq", bit) for bit in seq_bits] + [("expert", bit) for bit in group_bits]
    )
    gains = gather_parts(gain, "tensor", tensor_bits)
    w_in = jnp.concatenate([w_gate[0], w_up[0]], axis=1)

    paths = (group_bits, group_bits[::-1])
    gathered = []
    for n, rows_of in enumerate(attended):
        path = paths[n % len(paths)]
        held = gather_parts(rows_of, "expert", path)
        order = slot_order(path)
        gathered += [held[order.index(r)] for r in range(group_count)]

    def projected(k, kind):
        shape = (group_count, rows_here, piece)
        return local_kernel(
            functools.partial(project_kernel, k),
            [jax.ShapeDtypeStruct(shape, kind)],
            [out_weight, *gathered],
            [pltpu.VMEM((group_count * rows_here, out_weight.shape[0]), jnp.bfloat16)],
        )[0]

    terms = []
    for k in range(1, tensor_count):
        away = projected(k, jnp.bfloat16)
        terms.append(swap(away, "tensor", k))
    terms.append(projected(0, jnp.float32))
    rows = rows_here // CHUNKS
    part = jax.ShapeDtypeStruct((group_count, rows, piece), jnp.bfloat16)
    proj, *by_session = local_kernel(
        functools.partial(mix_kernel, group_count),
        [jax.ShapeDtypeStruct((group_count, rows_here, piece), jnp.float32)] + [part] * CHUNKS,
        [*x_slots, *terms],
    )
    w_in, table, *rest = lax.optimization_barrier((w_in, table, *gains, *by_session))
    gains, by_session = rest[:tensor_count], rest[tensor_count:]

    blocks = seq_count // 2
    chunks = []
    for c in range(CHUNKS):
        path = paths[c % len(paths)]
        held = by_session[c]
        held = gather_slots(held, "seq", far)
        held = gather_slots(held, "tensor", tensor_bits)
        own = gather_parts(held, "expert", path)
        other = []
        for part in own:
            other.append(swap(part, "seq", near[0]))
        chunks.append((c, path, own, other))

    def experts_on(c, path, parts, received):
        order = tuple(slot_order(path))
        operands = [table, w_in, w_down[0], *parts, *gains]
        shape = (tensor_count, blocks, rows, half_width)
        if received is None:
            shapes = [jax.ShapeDtypeStruct((group_count, *shape), jnp.bfloat16)]
        else:
            operands += [proj, received]
            shapes = [jax.ShapeDtypeStruct(shape, jnp.bfloat16)] * group_count
        near_order = near[0] if received is None else 0
        return local_kernel(
            functools.partial(expert_kernel, order, near_order, c * rows),
            shapes,
            operands,
            [
                pltpu.VMEM((group_count * blocks * rows, width), jnp.bfloat16),
                pltpu.VMEM((width // piece, piece), jnp.float32),
            ],
            KERNEL_BYTES,
        )

    finished = []
    for c, path, own, other in chunks:
        (away,) = experts_on(c, path, other, None)
        away = swap(away, "seq", near[0])
        parts = experts_on(c, path, own, away)
        terms = return_parts(parts, "expert", path)
        terms = return_rows(terms, "tensor", tensor_bits)
        terms = return_rows(terms, "seq", far)
        finished.append(sum(term.astype(jnp.float32) for term in terms))
    summed = jnp.concatenate(finished, axis=0)
    return (x_half.astype(jnp.float32) + summed).astype(jnp.bfloat16)[None]


def per_device(*arrays):
    rows_here = arrays[0].shape[1]
    counts = [lax.axis_size(axis) for axis in ("seq", "expert", "tensor")]
    experts = counts[0] * counts[1]
    capacity = max(2, 3 * rows_here * TOPK // (2 * experts))
    dense = experts * rows_here <= 2 * experts * capacity
    regular = all(count > 1 and count & (count - 1) == 0 for count in counts)
    fits = experts <= LANES and rows_here % (16 * CHUNKS) == 0
    if dense and regular and fits:
        return dense_plan(*arrays)
    return dispatch_plan(*arrays)


def solution(mesh):
    return jax.shard_map(
        per_device,
        mesh=mesh,
        in_specs=(
            P("expert", "seq", "tensor"),
            P("expert", "seq", "tensor"),
            P("expert", "seq", "tensor"),
            P("expert", "seq", None),
            P("tensor", "expert"),
            P("tensor"),
            P(("seq", "expert"), None, "tensor"),
            P(("seq", "expert"), None, "tensor"),
            P(("seq", "expert"), "tensor", None),
            P("expert", "seq", None),
            P("expert", "seq", None),
        ),
        out_specs=P("expert", "seq", "tensor"),
        check_vma=False,
    )
```

```python
import functools
import math

import jax
import jax.numpy as jnp
from jax import lax
from jax.experimental import pallas as pl
from jax.experimental.pallas import tpu as pltpu
from jax.sharding import PartitionSpec as P


HEAD_SIZE = 128
TOPK = 8
LANES = 128
CHUNKS = 4
KERNEL_BYTES = 6 << 20


def dispatch_plan(
    q_rows,
    k_rows,
    value_rows,
    x_rows,
    out_weight,
    norm_gain,
    w_gate,
    w_up,
    w_down,
    expert_ids,
    gate_weights,
):
    rows_here = q_rows.shape[1]
    kv_heads = k_rows.shape[2] // HEAD_SIZE
    q_heads = q_rows.shape[2] // HEAD_SIZE
    group_width = q_heads // kv_heads
    queries = q_rows[0].reshape(rows_here, kv_heads, group_width, HEAD_SIZE)
    offset = lax.axis_index("seq") * rows_here
    query_pos = offset + jnp.arange(rows_here, dtype=jnp.int32)
    softmax_scale = 1.0 / math.sqrt(HEAD_SIZE)
    tensor_pos = lax.axis_index("tensor")
    tensor_count = lax.axis_size("tensor")
    pieces = (
        lax.all_gather(k_rows, "seq", axis=1, tiled=True),
        lax.all_gather(value_rows, "seq", axis=1, tiled=True),
    )
    running_max = jnp.full((kv_heads, group_width, rows_here), -1e30, jnp.float32)
    block_rows = pieces[0].shape[1]
    key_block = pieces[0][0].reshape(block_rows, kv_heads, HEAD_SIZE)
    value_block = pieces[1][0].reshape(block_rows, kv_heads, HEAD_SIZE)
    scores = (
        jnp.einsum("igrd,jgd->grij", queries, key_block, preferred_element_type=jnp.float32)
        * softmax_scale
    )
    key_pos = jnp.arange(block_rows, dtype=jnp.int32)
    allowed = key_pos[None, :] <= query_pos[:, None]
    scores = jnp.where(allowed, scores, jnp.float32(-1e30))
    new_max = jnp.maximum(running_max, jnp.max(scores, axis=-1))
    weights = jnp.where(allowed, jnp.exp(scores - new_max[..., None]), jnp.float32(0.0))
    running_sum = jnp.sum(weights, axis=-1)
    weighted = jnp.einsum(
        "grij,jgd->grid",
        weights.astype(jnp.bfloat16),
        value_block,
        preferred_element_type=jnp.float32,
    )
    running_max, running_sum, weighted = (new_max, running_sum, weighted)
    attn_rows = (
        (weighted / running_sum[..., None])
        .transpose(2, 0, 1, 3)
        .reshape(rows_here, q_heads * HEAD_SIZE)
        .astype(jnp.bfloat16)
    )
    head_terms = jnp.dot(
        attn_rows,
        lax.all_gather(out_weight, "expert", axis=1, tiled=True),
        preferred_element_type=jnp.float32,
    )
    width = x_rows.shape[2]
    half_width = width // tensor_count
    share_sum = lax.psum_scatter(
        head_terms.astype(jnp.bfloat16), "tensor", scatter_dimension=1, tiled=True
    ).astype(jnp.float32)
    mixed_half = (
        lax.dynamic_slice_in_dim(x_rows[0], tensor_pos * half_width, half_width, 1).astype(
            jnp.float32
        )
        + share_sum
    )
    power = lax.psum(jnp.sum(mixed_half * mixed_half, axis=1), "tensor")
    inverse = lax.rsqrt(power / width + 1e-06)
    normed = (mixed_half * inverse[:, None] * norm_gain[None, :]).astype(jnp.bfloat16)
    seq_count = lax.axis_size("seq")
    group_count = lax.axis_size("expert")
    experts = seq_count * group_count
    capacity = max(2, 3 * rows_here * TOPK // (2 * experts))
    routed = expert_ids[0].reshape(-1)
    assigned = routed.shape[0]
    member = (routed[:, None] == jnp.arange(experts, dtype=jnp.int32)[None, :]).astype(jnp.int32)
    earlier = jnp.cumsum(member, axis=0) - member
    slot_index = jnp.sum(earlier * member, axis=1)
    target = routed * capacity + slot_index
    owner_index = (
        jnp.full((experts * capacity,), assigned, jnp.int32)
        .at[target]
        .set(jnp.arange(assigned, dtype=jnp.int32))
    )
    filled = owner_index < assigned
    source = jnp.minimum(owner_index // TOPK, rows_here - 1)
    outgoing = jnp.where(filled[:, None], normed[source], jnp.zeros((), jnp.bfloat16)).reshape(
        experts, capacity, half_width
    )
    arrived = lax.all_to_all(outgoing, ("seq", "expert"), split_axis=0, concat_axis=0, tiled=True)
    slot_count = arrived.shape[1]
    whole_rows = lax.all_gather(arrived, "tensor", axis=2, tiled=True)
    flat_rows = whole_rows.reshape(-1, whole_rows.shape[2])
    gate_act = jnp.dot(flat_rows, w_gate[0], preferred_element_type=jnp.float32)
    up_act = jnp.dot(flat_rows, w_up[0], preferred_element_type=jnp.float32)
    hidden = (jax.nn.silu(gate_act) * up_act).astype(jnp.bfloat16)
    partial_value = jnp.dot(hidden, w_down[0], preferred_element_type=jnp.float32).reshape(
        arrived.shape[0], slot_count, whole_rows.shape[2]
    )
    returned = lax.all_to_all(
        lax.psum_scatter(
            partial_value.astype(jnp.bfloat16), "tensor", scatter_dimension=2, tiled=True
        ),
        ("seq", "expert"),
        split_axis=0,
        concat_axis=0,
        tiled=True,
    )
    came_back = returned.reshape(experts * capacity, half_width)
    picked = came_back[target].astype(jnp.float32)
    weights_flat = gate_weights[0].reshape(-1)
    blended = jnp.sum((picked * weights_flat[:, None]).reshape(rows_here, TOPK, half_width), axis=1)
    return (mixed_half + blended).astype(jnp.bfloat16)[None]


def bits_of(size):
    return [1 << n for n in range(size.bit_length() - 1)]


def swap(value, axis, bit):
    count = lax.axis_size(axis)
    return lax.ppermute(value, axis, [(i, i ^ bit) for i in range(count)])


def slot_order(bits):
    order = [0]
    for bit in bits:
        order = order + [place ^ bit for place in order]
    return order


def gather_slots(value, axis, bits):
    held = value[None]
    for bit in bits:
        held = jnp.concatenate([held, swap(held, axis, bit)], axis=0)
    return held


def gather_parts(value, axis, bits):
    held = [value]
    for bit in bits:
        arrived = []
        for part in held:
            arrived.append(swap(part, axis, bit))
        held = held + arrived
    return held


def exchange_rows(table, steps):
    lanes = table.shape[1]
    sizes = {"seq": lax.axis_size("seq"), "expert": lax.axis_size("expert")}
    table = table.reshape(sizes["seq"], sizes["expert"], lanes)
    for axis, bit in steps:
        dim = 0 if axis == "seq" else 1
        size = sizes[axis]
        parts = jnp.split(table, size, axis=dim)
        low = [n for n in range(size) if not n & bit]
        away = jnp.concatenate([parts[n ^ bit] for n in low], axis=dim)
        away = swap(away, axis, bit)
        arrived = jnp.split(away, len(low), axis=dim)
        for n, part in zip(low, arrived):
            parts[n ^ bit] = part
        table = jnp.concatenate(parts, axis=dim)
    return table.reshape(-1, lanes)


def total(terms):
    if len(terms) == 1:
        return terms[0]
    return sum(term.astype(jnp.float32) for term in terms).astype(terms[0].dtype)


def return_parts(parts, axis, bits):
    held = [[part] for part in parts]
    for bit in reversed(bits):
        half = len(held) // 2
        arrived = [None] * half
        for i in reversed(range(half)):
            arrived[i] = swap(total(held[half + i]), axis, bit)
        held = [terms + [extra] for terms, extra in zip(held, arrived)]
    return held[0]


def return_rows(terms, axis, bits):
    for bit in reversed(bits):
        half = terms[0].shape[0] // 2
        arrived = swap(total([term[half:] for term in terms]), axis, bit)
        terms = [term[:half] for term in terms] + [arrived]
    return [term[0] for term in terms]


def expert_kernel(order, near, start_row, *refs):
    groups = len(order)
    refs = list(refs)
    table_ref, w_in_ref, w_out_ref = refs[:3]
    in_refs, refs = refs[3 : 3 + groups], refs[3 + groups :]
    halves, blocks, sessions, rows, piece = in_refs[0].shape
    gain_refs, refs = refs[:halves], refs[halves:]
    proj_ref, received_ref = (None, None) if near else (refs.pop(0), refs.pop(0))
    normed_ref, gain_ref = refs.pop(-2), refs.pop()
    half_width = refs[0].shape[-1]
    width = half_width * halves
    hidden_width = w_out_ref.shape[0]
    me, half_me = lax.axis_index("expert"), lax.axis_index("tensor")
    per_half = half_width // piece
    count = groups * rows * blocks
    for k, ref in enumerate(gain_refs):
        for n in range(per_half):
            for lane in range(0, piece, LANES):
                line = (n * piece + lane) // LANES
                gain_ref[k * per_half + n : k * per_half + n + 1, lane : lane + LANES] = ref[
                    line : line + 1
                ]

    power = jnp.zeros((count, 1), jnp.float32)
    pieces = []
    for i, in_ref in enumerate(in_refs):
        for k in range(halves):
            tokens = jnp.concatenate(
                [
                    in_ref[k, b, lax.bitwise_xor(me, order[r])]
                    for b in range(blocks)
                    for r in range(groups)
                ],
                axis=0,
            )
            mixed = tokens.astype(jnp.float32)
            power = power + jnp.sum(mixed * mixed, axis=1, keepdims=True)
            pieces.append((i, k, tokens))
    inverse = lax.rsqrt(power * (1.0 / width) + 1e-06)
    for i, k, tokens in pieces:
        spot = lax.bitwise_xor(me, order[i]) * halves + lax.bitwise_xor(half_me, k)
        away = lax.bitwise_xor(lax.div(spot, per_half), half_me)
        gain = gain_ref[pl.ds(away * per_half + lax.rem(spot, per_half), 1), :]
        normed_ref[:, pl.ds(pl.multiple_of(spot * piece, piece), piece)] = (
            tokens.astype(jnp.float32) * inverse * gain
        ).astype(jnp.bfloat16)
    both = jnp.dot(normed_ref[...], w_in_ref[...], preferred_element_type=jnp.float32)
    gate_act, up_act = both[:, :hidden_width], both[:, hidden_width:]
    hidden = (gate_act / (1.0 + jnp.exp(-gate_act)) * up_act).astype(jnp.bfloat16)

    diagonal = lax.broadcasted_iota(jnp.int32, (rows, rows), 0) == lax.broadcasted_iota(
        jnp.int32, (rows, rows), 1
    )
    scales = []
    for b in range(blocks):
        for r in range(groups):
            source = (2 * b + near) * sessions + order[r]
            line = table_ref[source : source + 1, start_row : start_row + rows]
            scales.append(
                jnp.sum(jnp.where(diagonal, line, 0.0), axis=1, keepdims=True)
            )
    scale = jnp.concatenate(scales, axis=0)
    for half in range(halves):
        k = lax.bitwise_xor(half_me, half)
        result = scale * jnp.dot(
            hidden,
            w_out_ref[:, half * half_width : (half + 1) * half_width],
            preferred_element_type=jnp.float32,
        )
        at = 0
        for b in range(blocks):
            for r in range(groups):
                part = result[at : at + rows]
                at += rows
                if proj_ref is not None and b == 0:
                    proj = proj_ref[order[r], start_row : start_row + rows]
                    columns = []
                    for m in range(per_half):
                        mine = me * halves + half_me == half * per_half + m
                        columns.append(
                            part[:, m * piece : (m + 1) * piece]
                            + proj * mine.astype(jnp.float32)
                        )
                    part = jnp.concatenate(columns, axis=1)
                if received_ref is not None:
                    part = part + received_ref[r, k, b].astype(jnp.float32)
                part = part.astype(jnp.bfloat16)
                if near:
                    refs[0][r, k, b] = part
                else:
                    refs[r][k, b] = part


def attention_kernel(head, order, q_ref, *refs):
    slots = len(order)
    k_refs, v_refs, out_ref = refs[:slots], refs[slots : 2 * slots], refs[-1]
    rows = q_ref.shape[0]
    columns = slice(head * HEAD_SIZE, (head + 1) * HEAD_SIZE)
    keys = jnp.concatenate([ref[:, columns] for ref in k_refs], axis=0)
    values = jnp.concatenate([ref[:, columns] for ref in v_refs], axis=0)
    down = lax.broadcasted_iota(jnp.int32, (rows, rows), 0)
    across = lax.broadcasted_iota(jnp.int32, (rows, rows), 1)
    seq_me = lax.axis_index("seq")
    allowed = jnp.concatenate(
        [
            (lax.bitwise_xor(seq_me, place) - seq_me) * rows + across <= down
            for place in order
        ],
        axis=1,
    )
    heads = out_ref.shape[1] // HEAD_SIZE
    batch = max(1, heads // 2)
    allowed = jnp.concatenate([allowed] * batch, axis=0)
    for first in range(0, heads, batch):
        queries = jnp.concatenate(
            [
                q_ref[:, (first + n) * HEAD_SIZE : (first + n + 1) * HEAD_SIZE]
                for n in range(batch)
            ],
            axis=0,
        )
        scores = lax.dot_general(
            queries, keys, (((1,), (1,)), ((), ())), preferred_element_type=jnp.float32
        ) * (1.0 / math.sqrt(HEAD_SIZE))
        scores = jnp.where(allowed, scores, jnp.float32(-1e30))
        weights = jnp.exp(scores - jnp.max(scores, axis=1, keepdims=True))
        mixed = jnp.dot(
            weights.astype(jnp.bfloat16), values, preferred_element_type=jnp.float32
        )
        mixed = (mixed / jnp.sum(weights, axis=1, keepdims=True)).astype(jnp.bfloat16)
        for n in range(batch):
            out_ref[:, (first + n) * HEAD_SIZE : (first + n + 1) * HEAD_SIZE] = mixed[
                n * rows : (n + 1) * rows
            ]


def side_kernel(groups, x_ref, q_ref, k_ref, v_ref, ids_ref, weights_ref, *refs):
    ids, weights, sems = refs[-3:]
    table_ref, half_ref, k_out, v_out = refs[:4]
    piece_refs, q_outs = refs[4 : 4 + groups], refs[4 + groups : -3]
    me, half_me, seq_me = (lax.axis_index(name) for name in ("expert", "tensor", "seq"))
    width, half_width, piece = (ref.shape[1] for ref in (x_ref, half_ref, piece_refs[0]))
    moves = [(ids_ref, ids), (weights_ref, weights)]
    for r, piece_ref in enumerate(piece_refs):
        spot = lax.bitwise_xor(me, r) * (width // half_width) + half_me
        start = pl.multiple_of(spot * piece, piece)
        moves.append((x_ref.at[:, pl.ds(start, piece)], piece_ref))
    moves += [(k_ref, k_out), (v_ref, v_out)]
    depth = q_outs[0].shape[1]
    for n, out in enumerate(q_outs):
        moves.append((q_ref.at[:, n * depth : (n + 1) * depth], out))
    start = pl.multiple_of(half_me * half_width, half_width)
    moves.append((x_ref.at[:, pl.ds(start, half_width)], half_ref))
    copies = [
        pltpu.make_async_copy(source, target, sems.at[n])
        for n, (source, target) in enumerate(moves)
    ]
    for copy in copies:
        copy.start()
    copies[0].wait()
    copies[1].wait()
    for n in range(table_ref.shape[0]):
        expert = lax.bitwise_xor(seq_me, n // groups) * groups
        expert = expert + lax.bitwise_xor(me, n % groups)
        table_ref[n : n + 1] = jnp.sum(
            jnp.where(ids[...] == expert, weights[...], 0.0), axis=0, keepdims=True
        )
    for copy in copies[2:]:
        copy.wait()


def project_kernel(away, w_ref, *refs):
    out_ref, joined_ref = refs[-2:]
    sessions, rows, piece = out_ref.shape
    depth = refs[0].shape[1]
    for n, ref in enumerate(refs[:-2]):
        half, r = divmod(n, sessions)
        joined_ref[r * rows : (r + 1) * rows, half * depth : (half + 1) * depth] = ref[...]
    start = pl.multiple_of(lax.bitwise_xor(lax.axis_index("tensor"), away) * piece, piece)
    result = jnp.dot(
        joined_ref[...], w_ref[:, pl.ds(start, piece)], preferred_element_type=jnp.float32
    )
    out_ref[...] = result.reshape(sessions, rows, piece).astype(out_ref.dtype)


def mix_kernel(groups, *refs):
    sessions = sum(len(slots) for slots in groups)
    x_refs, refs = refs[:sessions], refs[sessions:]
    terms, (proj_ref, *chunk_refs) = refs[: -1 - CHUNKS], refs[-1 - CHUNKS :]
    each = len(terms) // len(groups)
    rows = chunk_refs[0].shape[1]
    me = lax.axis_index("expert")
    for g, slots in enumerate(groups):
        for n, r in enumerate(slots):
            here = terms[g * each : (g + 1) * each]
            proj = sum(ref[n].astype(jnp.float32) for ref in here)
            proj_ref[r] = proj
            mixed = (x_refs[r][...].astype(jnp.float32) + proj).astype(jnp.bfloat16)
            for c, chunk_ref in enumerate(chunk_refs):
                chunk_ref[lax.bitwise_xor(me, r)] = mixed[c * rows : (c + 1) * rows]


def local_kernel(kernel, outs, operands, scratch=(), limit=8 << 20, space=pltpu.VMEM):
    return pl.pallas_call(
        kernel,
        out_shape=outs,
        in_specs=[pl.BlockSpec(memory_space=space)] * len(operands),
        out_specs=[pl.BlockSpec(memory_space=pltpu.VMEM)] * len(outs),
        scratch_shapes=scratch,
        compiler_params=pltpu.CompilerParams(vmem_limit_bytes=limit),
    )(*operands)


def dense_plan(
    q_rows,
    k_rows,
    value_rows,
    x_rows,
    out_weight,
    norm_gain,
    w_gate,
    w_up,
    w_down,
    expert_ids,
    gate_weights,
):
    rows_here = q_rows.shape[1]
    width = x_rows.shape[2]
    seq_count, group_count = lax.axis_size("seq"), lax.axis_size("expert")
    tensor_count = lax.axis_size("tensor")
    experts = seq_count * group_count
    seq_bits, group_bits = bits_of(seq_count), bits_of(group_count)
    tensor_bits = bits_of(tensor_count)
    half_width = width // tensor_count
    piece = width // (group_count * tensor_count)
    near, far = seq_bits[:1], seq_bits[1:]

    kv_bits = far + near
    keys = gather_parts(k_rows[0], "seq", kv_bits)
    values = gather_parts(value_rows[0], "seq", kv_bits)

    kv_heads = k_rows.shape[2] // HEAD_SIZE
    depth = q_rows.shape[2] // kv_heads
    kind = x_rows.dtype
    ids, weights = expert_ids[0].T, gate_weights[0].T
    shapes = [(experts, rows_here), (rows_here, half_width)]
    shapes += [k_rows.shape[1:]] * 2 + [(rows_here, piece)] * group_count
    shapes += [(rows_here, depth)] * kv_heads
    table, x_half, keys[0], values[0], *rest = local_kernel(
        functools.partial(side_kernel, group_count),
        [jax.ShapeDtypeStruct(shape, kind if n else jnp.float32) for n, shape in enumerate(shapes)],
        [
            pltpu.with_memory_space_constraint(value, pltpu.HBM)
            for value in (x_rows[0], q_rows[0], k_rows[0], value_rows[0], ids, weights)
        ],
        [
            pltpu.VMEM(ids.shape, ids.dtype),
            pltpu.VMEM(weights.shape, weights.dtype),
            pltpu.SemaphoreType.DMA((len(shapes) + 1,)),
        ],
        space=pltpu.HBM,
    )
    x_slots, queries = rest[:group_count], rest[group_count:]
    for r in range(1, group_count):
        x_slots[r] = swap(x_slots[r], "expert", r)
    gain = norm_gain.reshape(half_width // LANES, LANES)

    attended = []
    for head in range(kv_heads):
        attended += local_kernel(
            functools.partial(attention_kernel, head, tuple(slot_order(kv_bits))),
            [jax.ShapeDtypeStruct((rows_here, depth), jnp.bfloat16)],
            [queries[head], *keys, *values],
        )

    w_gate, w_up, gain, table, _ = lax.optimization_barrier(
        (w_gate, w_up, gain, table, attended[0])
    )
    table = exchange_rows(
        table, [("seq", bit) for bit in seq_bits] + [("expert", bit) for bit in group_bits]
    )
    gains = gather_parts(gain, "tensor", tensor_bits)
    w_in = jnp.concatenate([w_gate[0], w_up[0]], axis=1)

    paths = (group_bits, group_bits[::-1])
    gathered = []
    for n, rows_of in enumerate(attended):
        path = paths[n % len(paths)]
        held = gather_parts(rows_of, "expert", path)
        order = slot_order(path)
        gathered.append([held[order.index(r)] for r in range(group_count)])

    direct = [r for r in range(group_count) if not r & (r - 1)]
    groups = [direct, [r for r in range(group_count) if r not in direct]]

    def projected(k, g, kind):
        slots = groups[g]
        return local_kernel(
            functools.partial(project_kernel, k),
            [jax.ShapeDtypeStruct((len(slots), rows_here, piece), kind)],
            [out_weight] + [held[r] for held in gathered for r in slots],
            [pltpu.VMEM((len(slots) * rows_here, out_weight.shape[0]), jnp.bfloat16)],
        )[0]

    terms = []
    for g in range(len(groups)):
        for k in range(1, tensor_count):
            away = projected(k, g, jnp.bfloat16)
            terms.append(swap(away, "tensor", k))
        terms.append(projected(0, g, jnp.float32))
    rows = rows_here // CHUNKS
    part = jax.ShapeDtypeStruct((group_count, rows, piece), jnp.bfloat16)
    proj, *by_session = local_kernel(
        functools.partial(mix_kernel, groups),
        [jax.ShapeDtypeStruct((group_count, rows_here, piece), jnp.float32)] + [part] * CHUNKS,
        [*x_slots, *terms],
    )
    w_in, table, *rest = lax.optimization_barrier((w_in, table, *gains, *by_session))
    gains, by_session = rest[:tensor_count], rest[tensor_count:]

    blocks = seq_count // 2
    chunks = []
    for c in range(CHUNKS):
        path = paths[c % len(paths)]
        held = by_session[c]
        held = gather_slots(held, "seq", far)
        held = gather_slots(held, "tensor", tensor_bits)
        own = gather_parts(held, "expert", path)
        other = []
        for part in own:
            other.append(swap(part, "seq", near[0]))
        chunks.append((c, path, own, other))

    def experts_on(c, path, parts, received):
        order = tuple(slot_order(path))
        operands = [table, w_in, w_down[0], *parts, *gains]
        shape = (tensor_count, blocks, rows, half_width)
        if received is None:
            shapes = [jax.ShapeDtypeStruct((group_count, *shape), jnp.bfloat16)]
        else:
            operands += [proj, received]
            shapes = [jax.ShapeDtypeStruct(shape, jnp.bfloat16)] * group_count
        near_order = near[0] if received is None else 0
        return local_kernel(
            functools.partial(expert_kernel, order, near_order, c * rows),
            shapes,
            operands,
            [
                pltpu.VMEM((group_count * blocks * rows, width), jnp.bfloat16),
                pltpu.VMEM((width // piece, piece), jnp.float32),
            ],
            KERNEL_BYTES,
        )

    finished = []
    for c, path, own, other in chunks:
        (away,) = experts_on(c, path, other, None)
        away = swap(away, "seq", near[0])
        parts = experts_on(c, path, own, away)
        terms = return_parts(parts, "expert", path)
        terms = return_rows(terms, "tensor", tensor_bits)
        terms = return_rows(terms, "seq", far)
        finished.append(sum(term.astype(jnp.float32) for term in terms))
    summed = jnp.concatenate(finished, axis=0)
    return (x_half.astype(jnp.float32) + summed).astype(jnp.bfloat16)[None]


def per_device(*arrays):
    rows_here = arrays[0].shape[1]
    counts = [lax.axis_size(axis) for axis in ("seq", "expert", "tensor")]
    experts = counts[0] * counts[1]
    capacity = max(2, 3 * rows_here * TOPK // (2 * experts))
    dense = experts * rows_here <= 2 * experts * capacity
    regular = counts[1] > 2 and all(count > 1 and count & (count - 1) == 0 for count in counts)
    fits = experts <= LANES and rows_here % (16 * CHUNKS) == 0
    if dense and regular and fits:
        return dense_plan(*arrays)
    return dispatch_plan(*arrays)


def solution(mesh):
    return jax.shard_map(
        per_device,
        mesh=mesh,
        in_specs=(
            P("expert", "seq", "tensor"),
            P("expert", "seq", "tensor"),
            P("expert", "seq", "tensor"),
            P("expert", "seq", None),
            P("tensor", "expert"),
            P("tensor"),
            P(("seq", "expert"), None, "tensor"),
            P(("seq", "expert"), None, "tensor"),
            P(("seq", "expert"), "tensor", None),
            P("expert", "seq", None),
            P("expert", "seq", None),
        ),
        out_specs=P("expert", "seq", "tensor"),
        check_vma=False,
    )
```
